32 devices in a mesh: dp: 4 (over y, x), seq: 8 (over z, core).
Axes of the slice: x: 2, y: 2, z: 4, core: 2. Of those that a mesh axis runs over, the one named last changes fastest.
Arguments:
- tokens: bfloat16 [4, 2048, 2560], P('dp', 'seq'), may hold values from -6 to 6
- values: bfloat16 [4, 2048, 5120], P('dp', 'seq'), may hold values from -6 to 6
- out_grad: bfloat16 [4, 2048, 5120], P('dp', 'seq'), may hold values from -0.0029296875 to 0.0029296875
- w_bc: bfloat16 [2560, 256], replicated, may hold values from -0.009765625 to 0.009765625
- w_dt: bfloat16 [2560, 80], replicated, may hold values from -0.125 to 0.125
- a_log: float32 [80], replicated, may hold values from -13 to -2
- dt_bias: float32 [80], replicated, may hold values from -1 to 1
- fire_flags: int32 [4], P('dp'), may hold values from 0 to 1, as said below
- last_bc: float32 [4, 2560, 256], P('dp', 'seq'), may hold values from -27 to 27
- last_heads: float32 [4, 2, 80], P('dp'), may hold values from -6 to 6
- total_bc: float32 [2560, 256], P('seq'), may hold values from -6 to 6
- total_heads: float32 [2, 80], replicated, may hold values from -6 to 6
Outputs:
- new_total_bc: float32 [2560, 256], P('seq')
- new_total_heads: float32 [2, 80], replicated
- new_last_bc: float32 [4, 2560, 256], P('dp', 'seq')
- new_last_heads: float32 [4, 2, 80], P('dp')
- trigger: float32 [4], P('dp')
The draws below stay inside these ranges and needn't reach their ends.
Inputs may be any that keep to these rules, and one draw needn't show every extreme that they name: `fire_flags`: between 2 and 3 entries are 1; which ones varies.
All inputs are finite; a program needn't handle non-finite values.
Results may differ from the reference program's by a relative error of at most 0.0029.
Values sent between devices are 32-bit elements; how exact they have to be, the bound alone decides.
A program may use at most 320 MiB of HBM per device.

```python
import jax
import jax.numpy as jnp
from jax import lax

D = 2560
N = 128
H = 80
P_SIZE = 64
GROUP = 128
REPLICAS = 4
LENGTH = 2048


def draw_a_log(key, part):
    base_key = jax.random.fold_in(key, 101)
    pick_key, slow_key, fast_key = jax.random.split(base_key, 3)
    quick_heads = jax.random.permutation(pick_key, H) < H // 2
    slow_rate = jnp.exp(jax.random.uniform(slow_key, (H,), jnp.float32, jnp.log(0.3), jnp.log(2.0))) / LENGTH
    fast_rate = jnp.exp(jax.random.uniform(fast_key, (H,), jnp.float32, jnp.log(0.02), jnp.log(0.1)))
    return jnp.log(jnp.where(quick_heads, fast_rate, slow_rate)).astype(jnp.float32)


def draw_fire_flags(key, part):
    base_key = jax.random.fold_in(key, 202)
    count_key, order_key = jax.random.split(base_key, 2)
    fire_count = jax.random.randint(count_key, (), 2, REPLICAS)
    ranking = jax.random.permutation(order_key, REPLICAS)
    return (ranking < fire_count).astype(jnp.int32)


def draw_last_bc(key, part):
    base_key = jax.random.fold_in(key, 303)
    noise = jax.random.truncated_normal(base_key, -6.0, 6.0, (REPLICAS, D, 2 * N), jnp.float32)
    position = jnp.arange(D, dtype=jnp.float32) / (D - 1)
    row_scale = 0.5 * (1.0 + 2.0 * position)
    return (noise * row_scale[None, :, None]).astype(jnp.float32)


def strengthened(values, rng, source, target, parts, factor):
    owner, partner = [(jnp.arange(values.shape[dim]) // (values.shape[dim] // parts)).reshape([-1 if axis == dim else 1 for axis in range(values.ndim)]) for dim in (source, target)]
    chosen = jax.random.permutation(rng, parts)[partner]
    strong = (owner == chosen) | (owner == (partner + parts // 2) % parts)
    return jnp.where(strong, factor * values, values)


def level_of(stream_key, extent, shards, least, largest):
    def one(axis_at, blocks):
        steps = jax.random.uniform(jax.random.fold_in(jax.random.fold_in(stream_key, 6), axis_at), (blocks,), jnp.float32, least / len(shards), largest / len(shards))
        return jnp.repeat(jnp.exp(steps), extent[axis_at] // blocks).reshape((-1,) + (1,) * (len(extent) - axis_at - 1))

    loudness = one(*shards[0])
    for cut in shards[1:]:
        loudness = loudness * one(*cut)
    return loudness


def scatter_about(own_key, shape, width, reach, cuts=(), kind=jnp.bfloat16):
    factor_of = level_of(own_key, shape, cuts, -0.22, 0.18) if cuts else 1.0
    values = jax.random.normal(own_key, shape, jnp.float32) * width * factor_of
    return jnp.minimum(jnp.maximum(values, -reach), reach).astype(kind)


def noise_with(stream_key, extent, deviation, limit, shards, heavy, kind=jnp.bfloat16):
    drawn = deviation * jax.random.normal(stream_key, extent, jnp.float32)
    if shards:
        drawn = drawn * level_of(stream_key, extent, shards, -0.22, 0.18)
    return jnp.clip(strengthened(drawn, jax.random.fold_in(stream_key, 3), *heavy), -limit, limit).astype(kind)


def setup_inputs(seed: int = 0) -> dict:
    key_of = jax.random.split(jax.random.key(seed), 13)
    tokens = noise_with(key_of[0], (REPLICAS, LENGTH, D), 1.0, 6.0, ((0, 4), (1, 8)), (1, 2, 8, 2.0))
    values = scatter_about(key_of[1], (REPLICAS, LENGTH, H * P_SIZE), 1.0, 6.0, ((0, 4), (1, 8)))
    out_grad = scatter_about(key_of[2], (REPLICAS, LENGTH, H * P_SIZE), (1.0 / LENGTH), 0.0029296875, ((0, 4), (1, 8)))
    w_bc = scatter_about(key_of[3], (D, 2 * N), (D * N) ** -0.5, 0.009765625)
    w_dt = scatter_about(key_of[4], (D, H), D ** -0.5, 0.125)
    a_log = draw_a_log(jax.random.fold_in(key_of[12], 71), 0)
    dt_bias = jnp.clip(jax.random.uniform(key_of[6], (H,), jnp.float32, -1.0, 1.0), -1.0, 1.0)
    fire_flags = draw_fire_flags(jax.random.fold_in(key_of[12], 71), 0)
    last_bc = draw_last_bc(jax.random.fold_in(key_of[12], 71), 0)
    last_heads = scatter_about(key_of[9], (REPLICAS, 2, H), 1.0, 6.0, ((0, 4),), jnp.float32)
    total_bc = scatter_about(key_of[10], (D, 2 * N), 1.0, 6.0, ((0, 8),), jnp.float32)
    total_heads = scatter_about(key_of[11], (2, H), 1.0, 6.0, (), jnp.float32)
    return dict(tokens=tokens, values=values, out_grad=out_grad, w_bc=w_bc, w_dt=w_dt, a_log=a_log, dt_bias=dt_bias, fire_flags=fire_flags, last_bc=last_bc, last_heads=last_heads, total_bc=total_bc, total_heads=total_heads)


HIGHEST = lax.Precision.HIGHEST

def project_heads(projected, raw_dt, a_log, dt_bias):
    half_width = projected.shape[1] // 2
    step_rates = jax.nn.softplus(raw_dt + dt_bias)
    log_decay = -step_rates * jnp.exp(a_log)
    return (projected[:, :half_width], projected[:, half_width:], step_rates, log_decay)

def group_terms(carried, pieces):
    state_now, loss_sum = carried
    value_rows, b_rows, c_rows, step_rates, log_decay, grad_rows = pieces
    block_len, head_count = step_rates.shape
    values_full = value_rows.astype(jnp.float32).reshape(block_len, head_count, -1)
    grads_full = grad_rows.astype(jnp.float32).reshape(block_len, head_count, -1)
    cumulated = jnp.cumsum(log_decay, axis=0)
    decay_gap = cumulated.T[:, :, None] - cumulated.T[:, None, :]
    causal = lax.broadcasted_iota(jnp.int32, (block_len, block_len), 0) >= lax.broadcasted_iota(jnp.int32, (block_len, block_len), 1)
    decay_mat = jnp.exp(jnp.where(causal[None], decay_gap, -1e+30))
    scores = jnp.dot(c_rows, b_rows.T, precision=HIGHEST)
    mix_weights = decay_mat * scores[None] * step_rates.T[:, None, :]
    inside = jnp.einsum('hts,shp->thp', mix_weights, values_full, precision=HIGHEST)
    outside = jnp.einsum('tn,hnp->thp', c_rows, state_now, precision=HIGHEST) * jnp.exp(cumulated)[:, :, None]
    loss_sum = loss_sum + jnp.sum((inside + outside) * grads_full)
    tail_weight = jnp.exp(cumulated[-1] - cumulated) * step_rates
    fresh = jnp.einsum('sn,shp->hnp', b_rows, tail_weight[:, :, None] * values_full, precision=HIGHEST)
    state_now = jnp.exp(cumulated[-1])[:, None, None] * state_now + fresh
    return ((state_now, loss_sum), None)

def in_blocks(array):
    blocks = array.shape[0] // GROUP
    return array.reshape((blocks, GROUP) + array.shape[1:])

def sequence_loss(state_start, value_rows, b_rows, c_rows, step_rates, log_decay, grad_rows):
    pieces = (in_blocks(value_rows), in_blocks(b_rows), in_blocks(c_rows), in_blocks(step_rates), in_blocks(log_decay), in_blocks(grad_rows))
    carried, unused = lax.scan(jax.checkpoint(group_terms), (state_start, jnp.zeros((), jnp.float32)), pieces)
    return carried[1]

def replica_grads(tok_rows, value_rows, grad_rows, w_bc, w_dt, a_log, dt_bias):
    projected = jnp.dot(tok_rows, w_bc, preferred_element_type=jnp.float32)
    raw_dt = jnp.dot(tok_rows, w_dt, preferred_element_type=jnp.float32)

    def loss_of(projected, a_log, dt_bias):
        b_rows, c_rows, step_rates, log_decay = project_heads(projected, raw_dt, a_log, dt_bias)
        state_start = jnp.zeros((H, N, P_SIZE), jnp.float32)
        return sequence_loss(state_start, value_rows, b_rows, c_rows, step_rates, log_decay, grad_rows)
    loss_proj, loss_alog, loss_bias = jax.grad(loss_of, argnums=(0, 1, 2))(projected, a_log, dt_bias)
    grad_bc = jnp.einsum('td,tk->dk', tok_rows, loss_proj.astype(jnp.bfloat16), preferred_element_type=jnp.float32)
    return (grad_bc, jnp.stack([loss_alog, loss_bias]))

def reference(tokens, values, out_grad, w_bc, w_dt, a_log, dt_bias, fire_flags, last_bc, last_heads, total_bc, total_heads):
    fired_bc = jnp.zeros_like(total_bc)
    fired_heads = jnp.zeros_like(total_heads)
    kept_bc = []
    kept_heads = []
    norms = []
    for replica in range(REPLICAS):
        grad_bc, grad_heads = replica_grads(tokens[replica], values[replica], out_grad[replica], w_bc, w_dt, a_log, dt_bias)
        diff_bc = grad_bc - last_bc[replica]
        diff_heads = grad_heads - last_heads[replica]
        norms.append(jnp.sqrt(jnp.sum(diff_bc * diff_bc) + jnp.sum(diff_heads * diff_heads) + 1e-06))
        weight = fire_flags[replica].astype(jnp.float32)
        fired_bc = fired_bc + weight * diff_bc
        fired_heads = fired_heads + weight * diff_heads
        kept_bc.append(jnp.where(fire_flags[replica] > 0, grad_bc, last_bc[replica]))
        kept_heads.append(jnp.where(fire_flags[replica] > 0, grad_heads, last_heads[replica]))
    return (total_bc + fired_bc, total_heads + fired_heads, jnp.stack(kept_bc), jnp.stack(kept_heads), jnp.stack(norms))
```

```python
import functools

import jax
import jax.numpy as jnp
from jax import lax
from jax.experimental import pallas as pl
from jax.experimental.pallas import tpu as pltpu
from jax.sharding import PartitionSpec as P

GROUP = 128
LANES = 256
F32 = jnp.float32
BF16 = jnp.bfloat16
HIGHEST = lax.Precision.HIGHEST
MM = (((1,), (0,)), ((), ()))
NT = (((1,), (1,)), ((), ()))
TN = (((0,), (0,)), ((), ()))


def mm(a, b, dims=MM):
    return lax.dot_general(a, b, dims, preferred_element_type=F32)


def exact(a, b, dims=MM):
    return lax.dot_general(a, b, dims, precision=HIGHEST, preferred_element_type=F32)


def halves(x):
    hi = x.astype(BF16)
    return hi, (x - hi.astype(F32)).astype(BF16)


def mm3(a, b, dims=MM):
    return mm(a[0], b[0], dims) + (mm(a[0], b[1], dims) + mm(a[1], b[0], dims))


def spread(heads, lanes, per_head, first):
    row = lax.broadcasted_iota(jnp.int32, (heads, lanes), 0)
    lane = lax.broadcasted_iota(jnp.int32, (heads, lanes), 1)
    return (row == first + lane // per_head).astype(F32).astype(BF16)


def gathers(heads, lanes, per_head, first):
    lane = lax.broadcasted_iota(jnp.int32, (lanes, heads), 0)
    row = lax.broadcasted_iota(jnp.int32, (lanes, heads), 1)
    return (row == first + lane // per_head).astype(F32).astype(BF16)


def front_kernel(
    width, tok_ref, wbc_ref, wdt_ref, alog_ref, bias_ref, x_ref, g_ref,
    fresh_ref, entry_ref, proj_ref, cum_ref, rate_ref, sigcum_ref, sig_ref, dproj_ref, ra_ref, rb_ref,
    whi, wlo, cols, rows, score, dscore,
):
    k = pl.program_id(0)
    length, heads = cum_ref.shape
    half = proj_ref.shape[1] // 2
    blocks = length // GROUP
    pairs = [(i, j) for i in range(blocks) for j in range(i + 1)]

    @pl.when(k == 0)
    def _():
        tok = tok_ref[...]
        proj = mm(tok, wbc_ref[...])
        proj_ref[...] = proj
        z = mm(tok, wdt_ref[...]) + bias_ref[...]
        tail = jnp.exp(-jnp.abs(z))
        rate = jnp.maximum(z, 0.0) + jnp.log1p(tail)
        sig = jnp.where(z >= 0, 1.0, tail) / (1.0 + tail)
        speed = jnp.exp(alog_ref[...])
        tri = (
            lax.broadcasted_iota(jnp.int32, (length, length), 0)
            >= lax.broadcasted_iota(jnp.int32, (length, length), 1)
        ).astype(F32)
        cum = exact(tri, -rate * speed)
        sigcum = exact(tri, -sig * speed)
        cum_ref[...] = cum
        rate_ref[...] = rate
        sig_ref[...] = sig
        sigcum_ref[...] = sigcum
        for n, w in enumerate((jnp.exp(cum), jnp.exp(cum[length - 1 :] - cum) * rate)):
            hi, lo = halves(w)
            whi[n] = hi
            wlo[n] = lo
        hi, lo = halves(cum)
        cols[0] = hi
        cols[1] = lo
        cols[2] = (cum - hi.astype(F32) - lo.astype(F32)).astype(BF16)
        hi, lo = halves(sigcum)
        cols[3] = hi
        cols[4] = lo
        for n, w in enumerate((cum, rate, sigcum, sig)):
            rows[n] = w.T
        b, c = proj[:, :half], proj[:, half:]
        for n, (i, j) in enumerate(pairs):
            score[n] = exact(
                c[i * GROUP : (i + 1) * GROUP], b[j * GROUP : (j + 1) * GROUP], NT
            )
        dscore[...] = jnp.zeros_like(dscore)

    lanes = x_ref.shape[1]
    group = lanes // width
    first = k * group
    xs = x_ref[...]
    gs = g_ref[...]
    hot = spread(heads, lanes, width, first)
    grow = mm(whi[0], hot) + mm(wlo[0], hot)
    fade = mm(whi[1], hot) + mm(wlo[1], hot)
    proj = proj_ref[...]
    fresh_ref[0] = mm3(halves(proj[:, :half]), halves(fade * xs.astype(F32)), TN)
    entry_ref[0] = mm3(halves(proj[:, half:]), halves(grow * gs.astype(F32)), TN)
    causal = lax.broadcasted_iota(jnp.int32, (GROUP, GROUP), 0) >= lax.broadcasted_iota(
        jnp.int32, (GROUP, GROUP), 1
    )
    lane_head = lax.broadcasted_iota(jnp.int32, (GROUP, lanes), 1) // width
    for one in range(group):
        head = first + one
        pick = spread(heads, GROUP, GROUP, head)
        cum_col = mm(cols[0], pick) + (mm(cols[1], pick) + mm(cols[2], pick))
        sig_col = mm(cols[3], pick) + mm(cols[4], pick)
        at = pl.ds(head, 1)
        cum_row, rate_row, sc_row, sig_row = (rows[n, at, :] for n in range(4))
        ra = jnp.zeros((1, GROUP), F32)
        rb = jnp.zeros((1, GROUP), F32)
        lo_lane = (one * width) // GROUP * GROUP
        span = max(GROUP, width)
        gh = jnp.where(
            lane_head[:, lo_lane : lo_lane + span] == one, 1.0, 0.0
        ).astype(BF16)
        for n, (i, j) in enumerate(pairs):
            ti = slice(i * GROUP, (i + 1) * GROUP)
            sj = slice(j * GROUP, (j + 1) * GROUP)
            gap = cum_col[ti] - cum_row[:, sj]
            if i == j:
                gap = jnp.where(causal, gap, -1e30)
            inner = mm(
                gs[ti, lo_lane : lo_lane + span] * gh, xs[sj, lo_lane : lo_lane + span], NT
            )
            mixed = jnp.exp(gap) * inner
            dscore[n] += mixed * rate_row[:, sj]
            q = score[n] * mixed
            c0 = jnp.sum(q, axis=0, keepdims=True)
            if i == j:
                gap = jnp.where(causal, gap, 0.0)
            c1 = jnp.sum(q * gap, axis=0, keepdims=True)
            c2 = jnp.sum(q * sig_col[ti], axis=0, keepdims=True)
            ra += rate_row[:, sj] * c1
            rb += rate_row[:, sj] * (c2 - sc_row[:, sj] * c0) + sig_row[:, sj] * c0
        ra_ref[at, :] = ra
        rb_ref[at, :] = rb

    @pl.when(k == pl.num_programs(0) - 1)
    def _():
        proj = proj_ref[...]
        b, c = proj[:, :half], proj[:, half:]
        dproj_ref[...] = jnp.zeros_like(dproj_ref)
        for n, (i, j) in enumerate(pairs):
            ti = slice(i * GROUP, (i + 1) * GROUP)
            sj = slice(j * GROUP, (j + 1) * GROUP)
            d = halves(dscore[n])
            dproj_ref[ti, half:] += mm3(d, halves(b[sj]))
            dproj_ref[sj, :half] += mm3(d, halves(c[ti]), TN)


def chain_kernel(count, decay_ref, fresh_ref, entry_ref, state_ref, back_ref,
                 got_f, got_b, out_f, out_b, send_f, recv_f, send_b, recv_b):
    me = lax.axis_index("seq")
    chunks = fresh_ref.shape[0]
    right = lax.rem(me + 1, count)
    left = lax.rem(me + count - 1, count)
    barrier = pltpu.get_barrier_semaphore()
    for peer in (left, right):
        pl.semaphore_signal(
            barrier, inc=1, device_id={"seq": peer}, device_id_type=pl.DeviceIdType.MESH
        )
    pl.semaphore_wait(barrier, 2)

    def forward(k):
        return pltpu.make_async_remote_copy(
            src_ref=out_f.at[k], dst_ref=got_f.at[k], send_sem=send_f.at[k],
            recv_sem=recv_f.at[k], device_id={"seq": right},
            device_id_type=pl.DeviceIdType.MESH,
        )

    def backward(k):
        return pltpu.make_async_remote_copy(
            src_ref=out_b.at[k], dst_ref=got_b.at[k], send_sem=send_b.at[k],
            recv_sem=recv_b.at[k], device_id={"seq": left},
            device_id_type=pl.DeviceIdType.MESH,
        )

    def skew(place):
        return 3 * (place // 2) + place % 2

    ahead = skew(me)
    behind = skew(count - 1 - me)

    def step(tau, unused):
        k = tau - ahead

        @pl.when((k >= 0) & (k < chunks))
        def _():
            @pl.when(me == 0)
            def _():
                state_ref[k] = jnp.zeros(state_ref.shape[1:], F32)
                out_f[k] = fresh_ref[k]

            @pl.when(me > 0)
            def _():
                forward(k).wait_recv()
                value = got_f[k]
                state_ref[k] = value
                out_f[k] = decay_ref[k] * value + fresh_ref[k]

            @pl.when(me < count - 1)
            def _():
                forward(k).start()

        j = tau - behind

        @pl.when((j >= 0) & (j < chunks))
        def _():
            @pl.when(me == count - 1)
            def _():
                back_ref[j] = jnp.zeros(back_ref.shape[1:], F32)
                out_b[j] = entry_ref[j]

            @pl.when(me < count - 1)
            def _():
                backward(j).wait_recv()
                value = got_b[j]
                back_ref[j] = value
                out_b[j] = decay_ref[j] * value + entry_ref[j]

            @pl.when(me > 0)
            def _():
                backward(j).start()

        return unused

    lax.fori_loop(0, chunks + 3 * ((count - 1) // 2) + (count - 1) % 2, step, 0)

    def drain(k, unused):
        @pl.when(me < count - 1)
        def _():
            forward(k).wait_send()

        @pl.when(me > 0)
        def _():
            backward(k).wait_send()

        return unused

    lax.fori_loop(0, chunks, drain, 0)


def back_kernel(
    width, x_ref, g_ref, state_ref, back_ref, proj_ref, cum_ref, rate_ref, sigcum_ref, sig_ref,
    dproj_ref, ra_ref, rb_ref, out_ref, heads_ref, whi, wlo, he, hf, gacc, acc,
):
    k = pl.program_id(0)
    length, heads = cum_ref.shape
    half = proj_ref.shape[1] // 2

    @pl.when(k == 0)
    def _():
        cum = cum_ref[...]
        for n, w in enumerate((jnp.exp(cum), jnp.exp(cum[length - 1 :] - cum) * rate_ref[...])):
            hi, lo = halves(w)
            whi[n] = hi
            wlo[n] = lo
        he[...] = jnp.zeros_like(he)
        hf[...] = jnp.zeros_like(hf)
        gacc[...] = jnp.zeros_like(gacc)
        acc[...] = dproj_ref[...]

    lanes = x_ref.shape[1]
    first = k * (lanes // width)
    hot = spread(heads, lanes, width, first)
    cold = gathers(heads, lanes, width, first)
    xf = x_ref[...].astype(F32)
    gf = g_ref[...].astype(F32)
    state = state_ref[0]
    back = back_ref[0]
    state2 = halves(state)
    back2 = halves(back)
    proj = proj_ref[...]
    grow = mm(whi[0], hot) + mm(wlo[0], hot)
    fade = mm(whi[1], hot) + mm(wlo[1], hot)
    hi, lo = halves(gf * mm3(halves(proj[:, half:]), state2))
    he[...] += mm(hi, cold) + mm(lo, cold)
    hi, lo = halves(xf * mm3(halves(proj[:, :half]), back2))
    hf[...] += mm(hi, cold) + mm(lo, cold)
    acc[:, half:] += mm3(halves(grow * gf), state2, NT)
    acc[:, :half] += mm3(halves(fade * xf), back2, NT)
    both = jnp.broadcast_to(jnp.sum(state * back, axis=0, keepdims=True), (8, lanes))
    hi, lo = halves(both)
    gacc[...] += mm(hi, cold) + mm(lo, cold)

    @pl.when(k == pl.num_programs(0) - 1)
    def _():
        cum = cum_ref[...]
        sigcum = sigcum_ref[...]
        last = cum[length - 1 :]
        sig_last = sigcum[length - 1 :]
        e = jnp.exp(cum) * he[...]
        f0 = jnp.exp(last - cum) * hf[...]
        f = f0 * rate_ref[...]
        link = jnp.exp(last) * gacc[0:1, :]
        ga = jnp.sum(e * cum + f * (last - cum), axis=0, keepdims=True) + link * last
        gb = (
            jnp.sum(e * sigcum + f * (sig_last - sigcum) + f0 * sig_ref[...], axis=0, keepdims=True)
            + link * sig_last
        )
        heads_ref[0:1, :] = ga + jnp.sum(ra_ref[...].T, axis=0, keepdims=True)
        heads_ref[1:2, :] = gb + jnp.sum(rb_ref[...].T, axis=0, keepdims=True)
        out_ref[...] = acc[...].astype(BF16)


def local(
    count, tokens, values, out_grad, w_bc, w_dt, a_log, dt_bias, fire_flags,
    last_bc, last_heads, total_bc, total_heads,
):
    tok = tokens[0]
    x = values[0]
    g = out_grad[0]
    length, inner = x.shape
    heads = a_log.shape[0]
    width = inner // heads
    chunks = inner // LANES
    wide = w_bc.shape[1]
    half = wide // 2
    blocks = length // GROUP
    npairs = blocks * (blocks + 1) // 2
    sds = jax.ShapeDtypeStruct
    whole = lambda a: pl.BlockSpec(a.shape, lambda k: (0,) * len(a.shape))
    chunk2 = pl.BlockSpec((length, LANES), lambda k: (0, k))
    chunk3 = pl.BlockSpec((1, half, LANES), lambda k: (k, 0, 0))
    small = sds((length, heads), F32)
    states = sds((chunks, half, LANES), F32)
    outs = [states, states, sds((length, wide), F32), small, small, small, small,
            sds((length, wide), F32), sds((heads, GROUP), F32), sds((heads, GROUP), F32)]
    alog2 = a_log[None]
    bias2 = dt_bias[None]
    fresh, entry, proj, cum, rate, sigcum, sig, dproj, ra, rb = pl.pallas_call(
        functools.partial(front_kernel, width),
        grid=(chunks,),
        in_specs=[whole(tok), whole(w_bc), whole(w_dt), whole(alog2), whole(bias2), chunk2, chunk2],
        out_specs=[chunk3, chunk3] + [whole(o) for o in outs[2:]],
        out_shape=outs,
        scratch_shapes=[
            pltpu.VMEM((2, length, heads), BF16),
            pltpu.VMEM((2, length, heads), BF16),
            pltpu.VMEM((5, length, heads), BF16),
            pltpu.VMEM((4, heads, length), F32),
            pltpu.VMEM((npairs, GROUP, GROUP), F32),
            pltpu.VMEM((npairs, GROUP, GROUP), F32),
        ],
        name="front",
    )(tok, w_bc, w_dt, alog2, bias2, x, g)
    decay = jnp.repeat(jnp.exp(cum[length - 1]), width).reshape(chunks, 1, LANES)
    vm = pl.BlockSpec(memory_space=pltpu.VMEM)
    buf = pltpu.VMEM((chunks, half, LANES), F32)
    sem = pltpu.SemaphoreType.DMA((chunks,))
    state, back = pl.pallas_call(
        functools.partial(chain_kernel, count),
        in_specs=[vm, vm, vm],
        out_specs=[vm, vm],
        out_shape=[states, states],
        scratch_shapes=[buf, buf, buf, buf, sem, sem, sem, sem],
        compiler_params=pltpu.CompilerParams(
            collective_id=0, has_side_effects=True, vmem_limit_bytes=56 * 1024 * 1024
        ),
        name="chain",
    )(decay, fresh, entry)
    d_projected, grad_heads = pl.pallas_call(
        functools.partial(back_kernel, width),
        grid=(chunks,),
        in_specs=[chunk2, chunk2, chunk3, chunk3]
        + [whole(a) for a in (proj, cum, rate, sigcum, sig, dproj, ra, rb)],
        out_specs=[whole(proj), pl.BlockSpec((2, heads), lambda k: (0, 0))],
        out_shape=[sds((length, wide), BF16), sds((2, heads), F32)],
        scratch_shapes=[
            pltpu.VMEM((2, length, heads), BF16),
            pltpu.VMEM((2, length, heads), BF16),
            pltpu.VMEM((length, heads), F32),
            pltpu.VMEM((length, heads), F32),
            pltpu.VMEM((8, heads), F32),
            pltpu.VMEM((length, wide), F32),
        ],
        name="back",
    )(x, g, state, back, proj, cum, rate, sigcum, sig, dproj, ra, rb)
    grad_bc = mm(tok, d_projected, TN)
    own_last = last_bc[0]
    own_rows = lax.psum_scatter(grad_bc, "seq", scatter_dimension=0, tiled=True)
    diff_bc = own_rows - own_last
    square_bc, summed_heads = lax.psum((jnp.sum(diff_bc * diff_bc), grad_heads), "seq")
    diff_heads = summed_heads - last_heads[0]
    trigger = jnp.sqrt(square_bc + jnp.sum(diff_heads * diff_heads) + 1e-06)
    weight = fire_flags[0].astype(F32)
    fired_bc, fired_heads = lax.psum((weight * diff_bc, weight * diff_heads), "dp")
    new_total_bc = total_bc + fired_bc
    new_total_heads = total_heads + fired_heads
    new_last_bc = jnp.where(fire_flags[0] > 0, own_rows, own_last)[None]
    new_last_heads = jnp.where(fire_flags[0] > 0, summed_heads, last_heads[0])[None]
    return (new_total_bc, new_total_heads, new_last_bc, new_last_heads, trigger.reshape(1))


def solution(mesh):
    in_specs = (
        P("dp", "seq", None), P("dp", "seq", None), P("dp", "seq", None), P(), P(), P(), P(),
        P("dp"), P("dp", "seq", None), P("dp", None, None), P("seq", None), P(),
    )
    out_specs = (P("seq", None), P(), P("dp", "seq", None), P("dp", None, None), P("dp"))
    return jax.shard_map(
        functools.partial(local, mesh.shape["seq"]), mesh=mesh, in_specs=in_specs,
        out_specs=out_specs, check_vma=False,
    )
```

```python
import functools

import jax
import jax.numpy as jnp
from jax import lax
from jax.experimental import pallas as pl
from jax.experimental.pallas import tpu as pltpu
from jax.sharding import PartitionSpec as P

GROUP = 128
LANES = 256
F32 = jnp.float32
BF16 = jnp.bfloat16
HIGHEST = lax.Precision.HIGHEST
MM = (((1,), (0,)), ((), ()))
NT = (((1,), (1,)), ((), ()))
TN = (((0,), (0,)), ((), ()))


def mm(a, b, dims=MM):
    return lax.dot_general(a, b, dims, preferred_element_type=F32)


def exact(a, b, dims=MM):
    return lax.dot_general(a, b, dims, precision=HIGHEST, preferred_element_type=F32)


def halves(x):
    hi = x.astype(BF16)
    return hi, (x - hi.astype(F32)).astype(BF16)


def mm3(a, b, dims=MM):
    return mm(a[0], b[0], dims) + (mm(a[0], b[1], dims) + mm(a[1], b[0], dims))


def spread(heads, lanes, per_head, first):
    row = lax.broadcasted_iota(jnp.int32, (heads, lanes), 0)
    lane = lax.broadcasted_iota(jnp.int32, (heads, lanes), 1)
    return (row == first + lane // per_head).astype(F32).astype(BF16)


def gathers(heads, lanes, per_head, first):
    lane = lax.broadcasted_iota(jnp.int32, (lanes, heads), 0)
    row = lax.broadcasted_iota(jnp.int32, (lanes, heads), 1)
    return (row == first + lane // per_head).astype(F32).astype(BF16)


def front_kernel(
    width, tok_ref, wbc_ref, wdt_ref, alog_ref, bias_ref, x_ref, g_ref,
    fresh_ref, entry_ref, proj_ref, cum_ref, rate_ref, sigcum_ref, sig_ref, dproj_ref, ra_ref, rb_ref,
    whi, wlo, cols, rows, score, dscore,
):
    k = pl.program_id(0)
    length, heads = cum_ref.shape
    half = proj_ref.shape[1] // 2
    blocks = length // GROUP
    pairs = [(i, j) for i in range(blocks) for j in range(i + 1)]

    @pl.when(k == 0)
    def _():
        tok = tok_ref[...]
        proj = mm(tok, wbc_ref[...])
        proj_ref[...] = proj
        z = mm(tok, wdt_ref[...], NT) + bias_ref[...]
        tail = jnp.exp(-jnp.abs(z))
        rate = jnp.maximum(z, 0.0) + jnp.log1p(tail)
        sig = jnp.where(z >= 0, 1.0, tail) / (1.0 + tail)
        speed = jnp.exp(alog_ref[...])
        tri = (
            lax.broadcasted_iota(jnp.int32, (length, length), 0)
            >= lax.broadcasted_iota(jnp.int32, (length, length), 1)
        ).astype(F32)
        cum = exact(tri, -rate * speed)
        sigcum = exact(tri, -sig * speed)
        cum_ref[...] = cum
        rate_ref[...] = rate
        sig_ref[...] = sig
        sigcum_ref[...] = sigcum
        for n, w in enumerate((jnp.exp(cum), jnp.exp(cum[length - 1 :] - cum) * rate)):
            hi, lo = halves(w)
            whi[n] = hi
            wlo[n] = lo
        hi, lo = halves(cum)
        cols[0] = hi
        cols[1] = lo
        cols[2] = (cum - hi.astype(F32) - lo.astype(F32)).astype(BF16)
        hi, lo = halves(sigcum)
        cols[3] = hi
        cols[4] = lo
        for n, w in enumerate((cum, rate, sigcum, sig)):
            rows[n] = w.T
        b, c = proj[:, :half], proj[:, half:]
        for n, (i, j) in enumerate(pairs):
            score[n] = exact(
                c[i * GROUP : (i + 1) * GROUP], b[j * GROUP : (j + 1) * GROUP], NT
            )
        dscore[...] = jnp.zeros_like(dscore)

    lanes = x_ref.shape[1]
    group = lanes // width
    first = k * group
    xs = x_ref[...]
    gs = g_ref[...]
    hot = spread(heads, lanes, width, first)
    grow = mm(whi[0], hot) + mm(wlo[0], hot)
    fade = mm(whi[1], hot) + mm(wlo[1], hot)
    proj = proj_ref[...]
    fresh_ref[0] = mm3(halves(proj[:, :half]), halves(fade * xs.astype(F32)), TN)
    entry_ref[0] = mm3(halves(proj[:, half:]), halves(grow * gs.astype(F32)), TN)
    causal = lax.broadcasted_iota(jnp.int32, (GROUP, GROUP), 0) >= lax.broadcasted_iota(
        jnp.int32, (GROUP, GROUP), 1
    )
    lane_head = lax.broadcasted_iota(jnp.int32, (GROUP, lanes), 1) // width
    for one in range(group):
        head = first + one
        pick = spread(heads, GROUP, GROUP, head)
        cum_col = mm(cols[0], pick) + (mm(cols[1], pick) + mm(cols[2], pick))
        sig_col = mm(cols[3], pick) + mm(cols[4], pick)
        at = pl.ds(head, 1)
        cum_row, rate_row, sc_row, sig_row = (rows[n, at, :] for n in range(4))
        ra = jnp.zeros((1, GROUP), F32)
        rb = jnp.zeros((1, GROUP), F32)
        lo_lane = (one * width) // GROUP * GROUP
        span = max(GROUP, width)
        gh = jnp.where(
            lane_head[:, lo_lane : lo_lane + span] == one, 1.0, 0.0
        ).astype(BF16)
        for n, (i, j) in enumerate(pairs):
            ti = slice(i * GROUP, (i + 1) * GROUP)
            sj = slice(j * GROUP, (j + 1) * GROUP)
            gap = cum_col[ti] - cum_row[:, sj]
            if i == j:
                gap = jnp.where(causal, gap, -1e30)
            inner = mm(
                gs[ti, lo_lane : lo_lane + span] * gh, xs[sj, lo_lane : lo_lane + span], NT
            )
            mixed = jnp.exp(gap) * inner
            dscore[n] += mixed * rate_row[:, sj]
            q = score[n] * mixed
            c0 = jnp.sum(q, axis=0, keepdims=True)
            if i == j:
                gap = jnp.where(causal, gap, 0.0)
            c1 = jnp.sum(q * gap, axis=0, keepdims=True)
            c2 = jnp.sum(q * sig_col[ti], axis=0, keepdims=True)
            ra += rate_row[:, sj] * c1
            rb += rate_row[:, sj] * (c2 - sc_row[:, sj] * c0) + sig_row[:, sj] * c0
        ra_ref[at, :] = ra
        rb_ref[at, :] = rb

    @pl.when(k == pl.num_programs(0) - 1)
    def _():
        proj = proj_ref[...]
        b, c = proj[:, :half], proj[:, half:]
        dproj_ref[...] = jnp.zeros_like(dproj_ref)
        for n, (i, j) in enumerate(pairs):
            ti = slice(i * GROUP, (i + 1) * GROUP)
            sj = slice(j * GROUP, (j + 1) * GROUP)
            d = halves(dscore[n])
            dproj_ref[ti, half:] += mm3(d, halves(b[sj]))
            dproj_ref[sj, :half] += mm3(d, halves(c[ti]), TN)


def chain_kernel(count, decay_ref, fresh_ref, entry_ref, state_ref, back_ref,
                 got_f, got_b, out_f, out_b, send_f, recv_f, send_b, recv_b):
    me = lax.axis_index("seq")
    chunks = fresh_ref.shape[0]
    right = lax.rem(me + 1, count)
    left = lax.rem(me + count - 1, count)
    barrier = pltpu.get_barrier_semaphore()
    for peer in (left, right):
        pl.semaphore_signal(
            barrier, inc=1, device_id={"seq": peer}, device_id_type=pl.DeviceIdType.MESH
        )
    pl.semaphore_wait(barrier, 2)

    def forward(k):
        return pltpu.make_async_remote_copy(
            src_ref=out_f.at[k], dst_ref=got_f.at[k], send_sem=send_f.at[k],
            recv_sem=recv_f.at[k], device_id={"seq": right},
            device_id_type=pl.DeviceIdType.MESH,
        )

    def backward(k):
        return pltpu.make_async_remote_copy(
            src_ref=out_b.at[k], dst_ref=got_b.at[k], send_sem=send_b.at[k],
            recv_sem=recv_b.at[k], device_id={"seq": left},
            device_id_type=pl.DeviceIdType.MESH,
        )

    ahead = skew(me)
    behind = skew(count - 1 - me)

    def step(tau, unused):
        k = tau - ahead

        @pl.when((k >= 0) & (k < chunks))
        def _():
            @pl.when(me == 0)
            def _():
                state_ref[k] = jnp.zeros(state_ref.shape[1:], F32)
                out_f[k] = fresh_ref[k]

            @pl.when(me > 0)
            def _():
                forward(k).wait_recv()
                value = got_f[k]
                state_ref[k] = value
                out_f[k] = decay_ref[k] * value + fresh_ref[k]

            @pl.when(me < count - 1)
            def _():
                forward(k).start()

        j = tau - behind

        @pl.when((j >= 0) & (j < chunks))
        def _():
            @pl.when(me == count - 1)
            def _():
                back_ref[j] = jnp.zeros(back_ref.shape[1:], F32)
                out_b[j] = entry_ref[j]

            @pl.when(me < count - 1)
            def _():
                backward(j).wait_recv()
                value = got_b[j]
                back_ref[j] = value
                out_b[j] = decay_ref[j] * value + entry_ref[j]

            @pl.when(me > 0)
            def _():
                backward(j).start()

        return unused

    lax.fori_loop(0, chunks + 3 * ((count - 1) // 2) + (count - 1) % 2, step, 0)

    def drain(k, unused):
        @pl.when(me < count - 1)
        def _():
            forward(k).wait_send()

        @pl.when(me > 0)
        def _():
            backward(k).wait_send()

        return unused

    lax.fori_loop(0, chunks, drain, 0)


def back_kernel(
    width, x_ref, g_ref, state_ref, back_ref, proj_ref, cum_ref, rate_ref, sigcum_ref, sig_ref,
    dproj_ref, ra_ref, rb_ref, out_ref, heads_ref, whi, wlo, he, hf, gacc, acc,
):
    k = pl.program_id(0)
    length, heads = cum_ref.shape
    half = proj_ref.shape[1] // 2

    @pl.when(k == 0)
    def _():
        cum = cum_ref[...]
        for n, w in enumerate((jnp.exp(cum), jnp.exp(cum[length - 1 :] - cum) * rate_ref[...])):
            hi, lo = halves(w)
            whi[n] = hi
            wlo[n] = lo
        he[...] = jnp.zeros_like(he)
        hf[...] = jnp.zeros_like(hf)
        gacc[...] = jnp.zeros_like(gacc)
        acc[...] = dproj_ref[...]

    lanes = x_ref.shape[1]
    first = k * (lanes // width)
    hot = spread(heads, lanes, width, first)
    cold = gathers(heads, lanes, width, first)
    xf = x_ref[...].astype(F32)
    gf = g_ref[...].astype(F32)
    state = state_ref[0]
    back = back_ref[0]
    state2 = halves(state)
    back2 = halves(back)
    proj = proj_ref[...]
    grow = mm(whi[0], hot) + mm(wlo[0], hot)
    fade = mm(whi[1], hot) + mm(wlo[1], hot)
    hi, lo = halves(gf * mm3(halves(proj[:, half:]), state2))
    he[...] += mm(hi, cold) + mm(lo, cold)
    hi, lo = halves(xf * mm3(halves(proj[:, :half]), back2))
    hf[...] += mm(hi, cold) + mm(lo, cold)
    acc[:, half:] += mm3(halves(grow * gf), state2, NT)
    acc[:, :half] += mm3(halves(fade * xf), back2, NT)
    both = jnp.broadcast_to(jnp.sum(state * back, axis=0, keepdims=True), (8, lanes))
    hi, lo = halves(both)
    gacc[...] += mm(hi, cold) + mm(lo, cold)

    @pl.when(k == pl.num_programs(0) - 1)
    def _():
        cum = cum_ref[...]
        sigcum = sigcum_ref[...]
        last = cum[length - 1 :]
        sig_last = sigcum[length - 1 :]
        e = jnp.exp(cum) * he[...]
        f0 = jnp.exp(last - cum) * hf[...]
        f = f0 * rate_ref[...]
        link = jnp.exp(last) * gacc[0:1, :]
        ga = jnp.sum(e * cum + f * (last - cum), axis=0, keepdims=True) + link * last
        gb = (
            jnp.sum(e * sigcum + f * (sig_last - sigcum) + f0 * sig_ref[...], axis=0, keepdims=True)
            + link * sig_last
        )
        heads_ref[0:1, :] = ga + jnp.sum(ra_ref[...].T, axis=0, keepdims=True)
        heads_ref[1:2, :] = gb + jnp.sum(rb_ref[...].T, axis=0, keepdims=True)
        out_ref[...] = acc[...].astype(BF16)


def remote(src, dst, send, recv, axis, peer):
    return pltpu.make_async_remote_copy(
        src_ref=src, dst_ref=dst, send_sem=send, recv_sem=recv, device_id={axis: peer},
        device_id_type=pl.DeviceIdType.MESH,
    )


def skew(place):
    return 3 * (place // 2) + place % 2


def tail_kernel(
    count, replicas, tok_ref, dproj_ref, heads_ref, last_ref, last_heads_ref, weight_ref,
    rows_ref, fired_ref, sum_ref, fired_heads_ref, square_ref,
    own, got_r, got_l, pay, dgot, hgot, hmine, sgot, smine,
    send_r, recv_r, send_l, recv_l, send_d, recv_d, send_h, recv_h, send_s, recv_s,
):
    me = lax.axis_index("seq")
    mine = lax.axis_index("dp")
    rows = last_ref.shape[0]
    half = rows // 2
    wide = last_ref.shape[1]
    stages = replicas.bit_length() - 1

    def partner(bit):
        size = 2**bit
        return mine + size * (1 - 2 * (mine // size % 2))

    barrier = pltpu.get_barrier_semaphore()
    for d in range(1, count):
        pl.semaphore_signal(
            barrier, inc=1, device_id={"seq": lax.rem(me + d, count)},
            device_id_type=pl.DeviceIdType.MESH,
        )
    for bit in range(stages):
        pl.semaphore_signal(
            barrier, inc=1, device_id={"dp": partner(bit)}, device_id_type=pl.DeviceIdType.MESH
        )

    hmine[...] = heads_ref[...]
    hgot[me] = heads_ref[...]
    tok_rows = tok_ref.shape[1] // wide
    dproj = dproj_ref[...]
    for n in range(tok_rows):
        own[n * wide : (n + 1) * wide, :] = mm(tok_ref[:, n * wide : (n + 1) * wide], dproj, TN)
    pl.semaphore_wait(barrier, count - 1 + stages)

    def to_peer(d, src, got, send, recv):
        return remote(
            src, got.at[me], send.at[d], recv.at[me], "seq", lax.rem(me + d, count)
        )

    def from_peer(d, src, got, send, recv):
        place = lax.rem(me + d, count)
        return remote(src, got.at[place], send.at[d], recv.at[place], "seq", place)

    def block(j):
        return own.at[pl.ds(pl.multiple_of(j * rows, 8), rows)]

    def step(tau, unused):
        t = tau - skew(me)
        j = count - 1 - t

        @pl.when((t >= 0) & (j >= me))
        def _():
            ref = block(j)

            @pl.when(me > 0)
            def _():
                remote(ref, got_r.at[j], send_r.at[j], recv_r.at[j], "seq", me - 1).wait_recv()
                ref[...] += got_r[j]

            @pl.when(j > me)
            def _():
                remote(ref, got_r.at[j], send_r.at[j], recv_r.at[j], "seq", me + 1).start()

        u = tau - skew(count - 1 - me)

        @pl.when((u >= 0) & (u <= me))
        def _():
            ref = block(u)

            @pl.when(me < count - 1)
            def _():
                remote(ref, got_l.at[u], send_l.at[u], recv_l.at[u], "seq", me + 1).wait_recv()
                ref[...] += got_l[u]

            @pl.when(u < me)
            def _():
                remote(ref, got_l.at[u], send_l.at[u], recv_l.at[u], "seq", me - 1).start()

        return unused

    for d in range(1, count):
        to_peer(d, hmine, hgot, send_h, recv_h).start()
    lax.fori_loop(0, count + skew(count - 1), step, 0)

    for d in range(1, count):
        from_peer(d, hmine, hgot, send_h, recv_h).wait_recv()
    summed = hgot[0]
    for n in range(1, count):
        summed = summed + hgot[n]
    sum_ref[...] = summed
    own_rows = block(me)[...]
    rows_ref[...] = own_rows
    diff = own_rows - last_ref[...]
    square = jnp.sum(diff * diff, axis=0, keepdims=True)
    square = sum(square[:, n * GROUP : (n + 1) * GROUP] for n in range(wide // GROUP))
    square = jnp.broadcast_to(square, smine.shape)
    weight = weight_ref[0:1, :]
    weighted = diff * weight
    for h in range(2):
        pay[h, 0, :half, :] = weighted[h * half : (h + 1) * half]
        pay[h, 0, half:, :] = jnp.zeros((8, wide), F32)
    pay[0, 0, half:, :GROUP] = (summed - last_heads_ref[...]) * weight[:, :GROUP]

    def swap(h, s):
        bit = s if h == 0 else stages - 1 - s
        return remote(
            pay.at[h, s], dgot.at[h, s], send_d.at[h, s], recv_d.at[h, s], "dp", partner(bit)
        )

    for h in range(2):
        swap(h, 0).start()
    smine[...] = square
    sgot[me] = square
    for d in range(1, count):
        to_peer(d, smine, sgot, send_s, recv_s).start()
    for s in range(stages):
        for h in range(2):
            swap(h, s).wait_recv()
            pay[h, s + 1] = pay[h, s] + dgot[h, s]
            if s + 1 < stages:
                swap(h, s + 1).start()
    for h in range(2):
        fired_ref[h * half : (h + 1) * half, :] = pay[h, stages, :half, :]
    fired_heads_ref[...] = pay[0, stages, half:, :GROUP]
    for d in range(1, count):
        from_peer(d, smine, sgot, send_s, recv_s).wait_recv()
    total = sgot[0]
    for n in range(1, count):
        total = total + sgot[n]
    square_ref[...] = total

    for s in range(stages):
        for h in range(2):
            swap(h, s).wait_send()
    for d in range(1, count):
        to_peer(d, hmine, hgot, send_h, recv_h).wait_send()
        to_peer(d, smine, sgot, send_s, recv_s).wait_send()

    def drain(j, unused):
        @pl.when(j > me)
        def _():
            remote(block(j), got_r.at[j], send_r.at[j], recv_r.at[j], "seq", me + 1).wait_send()

        @pl.when(j < me)
        def _():
            remote(block(j), got_l.at[j], send_l.at[j], recv_l.at[j], "seq", me - 1).wait_send()

        return unused

    lax.fori_loop(0, count, drain, 0)


def local(
    count, replicas, tokens, values, out_grad, w_bc, w_dt, a_log, dt_bias, fire_flags,
    last_bc, last_heads, total_bc, total_heads,
):
    tok = tokens[0]
    x = values[0]
    g = out_grad[0]
    length, inner = x.shape
    heads = a_log.shape[0]
    width = inner // heads
    chunks = inner // LANES
    wide = w_bc.shape[1]
    half = wide // 2
    blocks = length // GROUP
    npairs = blocks * (blocks + 1) // 2
    sds = jax.ShapeDtypeStruct
    whole = lambda a: pl.BlockSpec(a.shape, lambda k: (0,) * len(a.shape))
    chunk2 = pl.BlockSpec((length, LANES), lambda k: (0, k))
    chunk3 = pl.BlockSpec((1, half, LANES), lambda k: (k, 0, 0))
    small = sds((length, heads), F32)
    states = sds((chunks, half, LANES), F32)
    outs = [states, states, sds((length, wide), F32), small, small, small, small,
            sds((length, wide), F32), sds((heads, GROUP), F32), sds((heads, GROUP), F32)]
    alog2 = a_log[None]
    bias2 = dt_bias[None]
    wdt = w_dt.T
    fresh, entry, proj, cum, rate, sigcum, sig, dproj, ra, rb = pl.pallas_call(
        functools.partial(front_kernel, width),
        grid=(chunks,),
        in_specs=[whole(tok), whole(w_bc), whole(wdt), whole(alog2), whole(bias2), chunk2, chunk2],
        out_specs=[chunk3, chunk3] + [whole(o) for o in outs[2:]],
        out_shape=outs,
        scratch_shapes=[
            pltpu.VMEM((2, length, heads), BF16),
            pltpu.VMEM((2, length, heads), BF16),
            pltpu.VMEM((5, length, heads), BF16),
            pltpu.VMEM((4, heads, length), F32),
            pltpu.VMEM((npairs, GROUP, GROUP), F32),
            pltpu.VMEM((npairs, GROUP, GROUP), F32),
        ],
        name="front",
    )(tok, w_bc, wdt, alog2, bias2, x, g)
    decay = jnp.repeat(jnp.exp(cum[length - 1]), width).reshape(chunks, 1, LANES)
    vm = pl.BlockSpec(memory_space=pltpu.VMEM)
    buf = pltpu.VMEM((chunks, half, LANES), F32)
    sem = pltpu.SemaphoreType.DMA((chunks,))
    state, back = pl.pallas_call(
        functools.partial(chain_kernel, count),
        in_specs=[vm, vm, vm],
        out_specs=[vm, vm],
        out_shape=[states, states],
        scratch_shapes=[buf, buf, buf, buf, sem, sem, sem, sem],
        compiler_params=pltpu.CompilerParams(
            collective_id=0, has_side_effects=True, vmem_limit_bytes=56 * 1024 * 1024
        ),
        name="chain",
    )(decay, fresh, entry)
    d_projected, grad_heads = pl.pallas_call(
        functools.partial(back_kernel, width),
        grid=(chunks,),
        in_specs=[chunk2, chunk2, chunk3, chunk3]
        + [whole(a) for a in (proj, cum, rate, sigcum, sig, dproj, ra, rb)],
        out_specs=[whole(proj), pl.BlockSpec((2, heads), lambda k: (0, 0))],
        out_shape=[sds((length, wide), BF16), sds((2, heads), F32)],
        scratch_shapes=[
            pltpu.VMEM((2, length, heads), BF16),
            pltpu.VMEM((2, length, heads), BF16),
            pltpu.VMEM((length, heads), F32),
            pltpu.VMEM((length, heads), F32),
            pltpu.VMEM((8, heads), F32),
            pltpu.VMEM((length, wide), F32),
        ],
        name="back",
    )(x, g, state, back, proj, cum, rate, sigcum, sig, dproj, ra, rb)
    own_last = last_bc[0]
    rows = own_last.shape[0]
    stages = replicas.bit_length() - 1
    tile = lambda a: jnp.pad(a, ((0, 8 - a.shape[0]), (0, GROUP - a.shape[1])))
    weight = jnp.broadcast_to(fire_flags[0].astype(F32), (8, wide))
    dma = pltpu.SemaphoreType.DMA
    own_rows, fired_bc, summed, fired, square = pl.pallas_call(
        functools.partial(tail_kernel, count, replicas),
        in_specs=[vm] * 6,
        out_specs=[vm] * 5,
        out_shape=[sds((rows, wide), F32)] * 2 + [sds((8, GROUP), F32)] * 3,
        scratch_shapes=[
            pltpu.VMEM((rows * count, wide), F32),
            pltpu.VMEM((count, rows, wide), F32),
            pltpu.VMEM((count, rows, wide), F32),
            pltpu.VMEM((2, stages + 1, rows // 2 + 8, wide), F32),
            pltpu.VMEM((2, stages, rows // 2 + 8, wide), F32),
            pltpu.VMEM((count, 8, GROUP), F32),
            pltpu.VMEM((8, GROUP), F32),
            pltpu.VMEM((count, 8, GROUP), F32),
            pltpu.VMEM((8, GROUP), F32),
        ]
        + [dma((count,))] * 4 + [dma((2, stages))] * 2 + [dma((count,))] * 4,
        compiler_params=pltpu.CompilerParams(
            collective_id=1, has_side_effects=True, vmem_limit_bytes=48 * 1024 * 1024
        ),
        name="tail",
    )(tok, d_projected, tile(grad_heads), own_last, tile(last_heads[0]), weight)
    summed_heads = summed[:2, :heads]
    diff_heads = summed_heads - last_heads[0]
    trigger = jnp.sqrt(jnp.sum(square[0]) + jnp.sum(diff_heads * diff_heads) + 1e-06)
    new_total_bc = total_bc + fired_bc
    new_total_heads = total_heads + fired[:2, :heads]
    new_last_bc = jnp.where(fire_flags[0] > 0, own_rows, own_last)[None]
    new_last_heads = jnp.where(fire_flags[0] > 0, summed_heads, last_heads[0])[None]
    return (new_total_bc, new_total_heads, new_last_bc, new_last_heads, trigger.reshape(1))


def solution(mesh):
    in_specs = (
        P("dp", "seq", None), P("dp", "seq", None), P("dp", "seq", None), P(), P(), P(), P(),
        P("dp"), P("dp", "seq", None), P("dp", None, None), P("seq", None), P(),
    )
    out_specs = (P("seq", None), P(), P("dp", "seq", None), P("dp", None, None), P("dp"))
    return jax.shard_map(
        functools.partial(local, mesh.shape["seq"], mesh.shape["dp"]), mesh=mesh, in_specs=in_specs,
        out_specs=out_specs, check_vma=False,
    )
```

```python
import functools

import jax
import jax.numpy as jnp
from jax import lax
from jax.experimental import pallas as pl
from jax.experimental.pallas import tpu as pltpu
from jax.sharding import PartitionSpec as P

GROUP = 128
LANES = 256
F32 = jnp.float32
BF16 = jnp.bfloat16
HIGHEST = lax.Precision.HIGHEST
MM = (((1,), (0,)), ((), ()))
NT = (((1,), (1,)), ((), ()))
TN = (((0,), (0,)), ((), ()))


def mm(a, b, dims=MM):
    return lax.dot_general(a, b, dims, preferred_element_type=F32)


def exact(a, b, dims=MM):
    return lax.dot_general(a, b, dims, precision=HIGHEST, preferred_element_type=F32)


def halves(x):
    hi = x.astype(BF16)
    return hi, (x - hi.astype(F32)).astype(BF16)


def mm3(a, b, dims=MM):
    return mm(a[0], b[0], dims) + (mm(a[0], b[1], dims) + mm(a[1], b[0], dims))


def spread(heads, lanes, per_head, first):
    row = lax.broadcasted_iota(jnp.int32, (heads, lanes), 0)
    lane = lax.broadcasted_iota(jnp.int32, (heads, lanes), 1)
    return (row == first + lane // per_head).astype(F32).astype(BF16)


def gathers(heads, lanes, per_head, first):
    lane = lax.broadcasted_iota(jnp.int32, (lanes, heads), 0)
    row = lax.broadcasted_iota(jnp.int32, (lanes, heads), 1)
    return (row == first + lane // per_head).astype(F32).astype(BF16)


def front_kernel(
    width, tok_ref, wbc_ref, wdt_ref, alog_ref, bias_ref, x_ref, g_ref,
    fresh_ref, entry_ref, decay_ref, proj_ref, cum_ref, rate_ref, sigcum_ref, sig_ref, whi, wlo,
):
    k = pl.program_id(0)
    length, heads = cum_ref.shape
    half = proj_ref.shape[1] // 2

    @pl.when(k == 0)
    def _():
        tok = tok_ref[...]
        proj_ref[...] = mm(tok, wbc_ref[...])
        z = mm(tok, wdt_ref[...], NT) + bias_ref[...]
        tail = jnp.exp(-jnp.abs(z))
        rate = jnp.maximum(z, 0.0) + jnp.log1p(tail)
        sig = jnp.where(z >= 0, 1.0, tail) / (1.0 + tail)
        speed = jnp.exp(alog_ref[...])
        tri = (
            lax.broadcasted_iota(jnp.int32, (length, length), 0)
            >= lax.broadcasted_iota(jnp.int32, (length, length), 1)
        ).astype(F32)
        cum = exact(tri, -rate * speed)
        cum_ref[...] = cum
        rate_ref[...] = rate
        sig_ref[...] = sig
        sigcum_ref[...] = exact(tri, -sig * speed)
        for n, w in enumerate((jnp.exp(cum), jnp.exp(cum[length - 1 :] - cum) * rate)):
            hi, lo = halves(w)
            whi[n] = hi
            wlo[n] = lo

    lanes = x_ref.shape[1]
    hot = spread(heads, lanes, width, k * (lanes // width))
    grow = mm(whi[0], hot) + mm(wlo[0], hot)
    fade = mm(whi[1], hot) + mm(wlo[1], hot)
    decay_ref[0] = grow[length - 1 :]
    proj = proj_ref[...]
    fresh_ref[0] = mm3(halves(proj[:, :half]), halves(fade * x_ref[...].astype(F32)), TN)
    entry_ref[0] = mm3(halves(proj[:, half:]), halves(grow * g_ref[...].astype(F32)), TN)


def chain_kernel(
    count, width, decay_ref, fresh_ref, entry_ref, x_ref, g_ref,
    proj_ref, cum_ref, rate_ref, sigcum_ref, sig_ref, out_ref, heads_ref,
    got_f, got_b, out_f, out_b, whi, wlo, he, hf, gacc, acc, cols, rows, score, dscore,
    ra_ref, rb_ref, send_f, recv_f, send_b, recv_b,
):
    me = lax.axis_index("seq")
    chunks, half, lanes = fresh_ref.shape
    length, heads = cum_ref.shape
    blocks = length // GROUP
    pairs = [(i, j) for i in range(blocks) for j in range(i + 1)]
    group = lanes // width
    right = lax.rem(me + 1, count)
    left = lax.rem(me + count - 1, count)
    barrier = pltpu.get_barrier_semaphore()
    for peer in (left, right):
        pl.semaphore_signal(
            barrier, inc=1, device_id={"seq": peer}, device_id_type=pl.DeviceIdType.MESH
        )

    proj = proj_ref[...]
    b, c = proj[:, :half], proj[:, half:]
    cum = cum_ref[...]
    for n, w in enumerate((jnp.exp(cum), jnp.exp(cum[length - 1 :] - cum) * rate_ref[...])):
        hi, lo = halves(w)
        whi[n] = hi
        wlo[n] = lo
    hi, lo = halves(cum)
    cols[0] = hi
    cols[1] = lo
    cols[2] = (cum - hi.astype(F32) - lo.astype(F32)).astype(BF16)
    hi, lo = halves(sigcum_ref[...])
    cols[3] = hi
    cols[4] = lo
    for n, w in enumerate((cum_ref, rate_ref, sigcum_ref, sig_ref)):
        rows[n] = w[...].T
    for n, (i, j) in enumerate(pairs):
        score[n] = exact(c[i * GROUP : (i + 1) * GROUP], b[j * GROUP : (j + 1) * GROUP], NT)
    dscore[...] = jnp.zeros_like(dscore)
    he[...] = jnp.zeros_like(he)
    hf[...] = jnp.zeros_like(hf)
    gacc[...] = jnp.zeros_like(gacc)
    acc[...] = jnp.zeros_like(acc)
    pl.semaphore_wait(barrier, 2)

    def forward(k):
        return remote(out_f.at[k], got_f.at[k], send_f.at[k], recv_f.at[k], "seq", right)

    def backward(k):
        return remote(out_b.at[k], got_b.at[k], send_b.at[k], recv_b.at[k], "seq", left)

    def columns(k):
        return pl.ds(pl.multiple_of(k * lanes, lanes), lanes)

    def inner_terms(k):
        xs = x_ref[:, columns(k)]
        gs = g_ref[:, columns(k)]
        causal = lax.broadcasted_iota(jnp.int32, (GROUP, GROUP), 0) >= lax.broadcasted_iota(
            jnp.int32, (GROUP, GROUP), 1
        )
        lane_head = lax.broadcasted_iota(jnp.int32, (GROUP, lanes), 1) // width
        span = max(GROUP, width)
        for one in range(group):
            head = k * group + one
            pick = spread(heads, GROUP, GROUP, head)
            cum_col = mm(cols[0], pick) + (mm(cols[1], pick) + mm(cols[2], pick))
            sig_col = mm(cols[3], pick) + mm(cols[4], pick)
            at = pl.ds(head, 1)
            cum_row, rate_row, sc_row, sig_row = (rows[n, at, :] for n in range(4))
            ra = jnp.zeros((1, GROUP), F32)
            rb = jnp.zeros((1, GROUP), F32)
            low = (one * width) // GROUP * GROUP
            own = jnp.where(lane_head[:, low : low + span] == one, 1.0, 0.0).astype(BF16)
            for n, (i, j) in enumerate(pairs):
                ti = slice(i * GROUP, (i + 1) * GROUP)
                sj = slice(j * GROUP, (j + 1) * GROUP)
                gap = cum_col[ti] - cum_row[:, sj]
                if i == j:
                    gap = jnp.where(causal, gap, -1e30)
                inner = mm(gs[ti, low : low + span] * own, xs[sj, low : low + span], NT)
                mixed = jnp.exp(gap) * inner
                dscore[n] += mixed * rate_row[:, sj]
                q = score[n] * mixed
                c0 = jnp.sum(q, axis=0, keepdims=True)
                if i == j:
                    gap = jnp.where(causal, gap, 0.0)
                c1 = jnp.sum(q * gap, axis=0, keepdims=True)
                c2 = jnp.sum(q * sig_col[ti], axis=0, keepdims=True)
                ra += rate_row[:, sj] * c1
                rb += rate_row[:, sj] * (c2 - sc_row[:, sj] * c0) + sig_row[:, sj] * c0
            ra_ref[at, :] = ra
            rb_ref[at, :] = rb

    def outer_terms(k):
        hot = spread(heads, lanes, width, k * group)
        cold = gathers(heads, lanes, width, k * group)
        xf = x_ref[:, columns(k)].astype(F32)
        gf = g_ref[:, columns(k)].astype(F32)
        state = got_f[k]
        back = got_b[k]
        state2 = halves(state)
        back2 = halves(back)
        proj = proj_ref[...]
        grow = mm(whi[0], hot) + mm(wlo[0], hot)
        fade = mm(whi[1], hot) + mm(wlo[1], hot)
        hi, lo = halves(gf * mm3(halves(proj[:, half:]), state2))
        he[...] += mm(hi, cold) + mm(lo, cold)
        hi, lo = halves(xf * mm3(halves(proj[:, :half]), back2))
        hf[...] += mm(hi, cold) + mm(lo, cold)
        acc[:, half:] += mm3(halves(grow * gf), state2, NT)
        acc[:, :half] += mm3(halves(fade * xf), back2, NT)
        both = jnp.broadcast_to(jnp.sum(state * back, axis=0, keepdims=True), (8, lanes))
        hi, lo = halves(both)
        gacc[...] += mm(hi, cold) + mm(lo, cold)

    lead = skew(count - 1)
    each = pl.cdiv(chunks, lead)
    ahead = skew(me)
    behind = skew(count - 1 - me)

    def step(tau, unused):
        k = tau - ahead

        @pl.when((k >= 0) & (k < chunks))
        def _():
            @pl.when(me == 0)
            def _():
                got_f[k] = jnp.zeros((half, lanes), F32)
                out_f[k] = fresh_ref[k]

            @pl.when(me > 0)
            def _():
                forward(k).wait_recv()

                @pl.when(me < count - 1)
                def _():
                    out_f[k] = decay_ref[k] * got_f[k] + fresh_ref[k]

            @pl.when(me < count - 1)
            def _():
                forward(k).start()

        j = tau - behind

        @pl.when((j >= 0) & (j < chunks))
        def _():
            @pl.when(me == count - 1)
            def _():
                got_b[j] = jnp.zeros((half, lanes), F32)
                out_b[j] = entry_ref[j]

            @pl.when(me < count - 1)
            def _():
                backward(j).wait_recv()

                @pl.when(me > 0)
                def _():
                    out_b[j] = decay_ref[j] * got_b[j] + entry_ref[j]

            @pl.when(me > 0)
            def _():
                backward(j).start()

        @pl.when(tau < lead)
        def _():
            for n in range(each):
                item = tau * each + n

                @pl.when(item < chunks)
                def _():
                    inner_terms(item)

        @pl.when(tau >= lead)
        def _():
            outer_terms(tau - lead)

        return unused

    lax.fori_loop(0, chunks + lead, step, 0)

    for n, (i, j) in enumerate(pairs):
        ti = slice(i * GROUP, (i + 1) * GROUP)
        sj = slice(j * GROUP, (j + 1) * GROUP)
        d = halves(dscore[n])
        acc[ti, half:] += mm3(d, halves(b[sj]))
        acc[sj, :half] += mm3(d, halves(c[ti]), TN)
    out_ref[...] = acc[...].astype(BF16)
    sigcum = sigcum_ref[...]
    last = cum[length - 1 :]
    sig_last = sigcum[length - 1 :]
    e = jnp.exp(cum) * he[...]
    f0 = jnp.exp(last - cum) * hf[...]
    f = f0 * rate_ref[...]
    link = jnp.exp(last) * gacc[0:1, :]
    ga = jnp.sum(e * cum + f * (last - cum), axis=0, keepdims=True) + link * last
    gb = (
        jnp.sum(e * sigcum + f * (sig_last - sigcum) + f0 * sig_ref[...], axis=0, keepdims=True)
        + link * sig_last
    )
    heads_ref[...] = jnp.zeros_like(heads_ref)
    heads_ref[0:1, :heads] = ga + jnp.sum(ra_ref[...].T, axis=0, keepdims=True)
    heads_ref[1:2, :heads] = gb + jnp.sum(rb_ref[...].T, axis=0, keepdims=True)

    def drain(k, unused):
        @pl.when(me < count - 1)
        def _():
            forward(k).wait_send()

        @pl.when(me > 0)
        def _():
            backward(k).wait_send()

        return unused

    lax.fori_loop(0, chunks, drain, 0)


def remote(src, dst, send, recv, axis, peer):
    return pltpu.make_async_remote_copy(
        src_ref=src, dst_ref=dst, send_sem=send, recv_sem=recv, device_id={axis: peer},
        device_id_type=pl.DeviceIdType.MESH,
    )


def skew(place):
    return 3 * (place // 2) + place % 2


def tail_kernel(
    count, replicas, tok_ref, dproj_ref, heads_ref, last_ref, last_heads_ref, weight_ref,
    rows_ref, fired_ref, sum_ref, fired_heads_ref, square_ref,
    own, got_r, got_l, pay, dgot, hgot, hmine, sgot, smine,
    send_r, recv_r, send_l, recv_l, send_d, recv_d, send_h, recv_h, send_s, recv_s,
):
    me = lax.axis_index("seq")
    mine = lax.axis_index("dp")
    rows = last_ref.shape[0]
    half = rows // 2
    wide = last_ref.shape[1]
    stages = replicas.bit_length() - 1

    def partner(bit):
        size = 2**bit
        return mine + size * (1 - 2 * (mine // size % 2))

    barrier = pltpu.get_barrier_semaphore()
    for d in range(1, count):
        pl.semaphore_signal(
            barrier, inc=1, device_id={"seq": lax.rem(me + d, count)},
            device_id_type=pl.DeviceIdType.MESH,
        )
    for bit in range(stages):
        pl.semaphore_signal(
            barrier, inc=1, device_id={"dp": partner(bit)}, device_id_type=pl.DeviceIdType.MESH
        )

    hmine[...] = heads_ref[...]
    hgot[me] = heads_ref[...]
    tok_rows = tok_ref.shape[1] // wide
    dproj = dproj_ref[...]
    for n in range(tok_rows):
        own[n * wide : (n + 1) * wide, :] = mm(tok_ref[:, n * wide : (n + 1) * wide], dproj, TN)
    pl.semaphore_wait(barrier, count - 1 + stages)

    def to_peer(d, src, got, send, recv):
        return remote(
            src, got.at[me], send.at[d], recv.at[me], "seq", lax.rem(me + d, count)
        )

    def from_peer(d, src, got, send, recv):
        place = lax.rem(me + d, count)
        return remote(src, got.at[place], send.at[d], recv.at[place], "seq", place)

    def block(j):
        return own.at[pl.ds(pl.multiple_of(j * rows, 8), rows)]

    def step(tau, unused):
        t = tau - skew(me)
        j = count - 1 - t

        @pl.when((t >= 0) & (j >= me))
        def _():
            ref = block(j)

            @pl.when(me > 0)
            def _():
                remote(ref, got_r.at[j], send_r.at[j], recv_r.at[j], "seq", me - 1).wait_recv()
                ref[...] += got_r[j]

            @pl.when(j > me)
            def _():
                remote(ref, got_r.at[j], send_r.at[j], recv_r.at[j], "seq", me + 1).start()

        u = tau - skew(count - 1 - me)

        @pl.when((u >= 0) & (u <= me))
        def _():
            ref = block(u)

            @pl.when(me < count - 1)
            def _():
                remote(ref, got_l.at[u], send_l.at[u], recv_l.at[u], "seq", me + 1).wait_recv()
                ref[...] += got_l[u]

            @pl.when(u < me)
            def _():
                remote(ref, got_l.at[u], send_l.at[u], recv_l.at[u], "seq", me - 1).start()

        return unused

    for d in range(1, count):
        to_peer(d, hmine, hgot, send_h, recv_h).start()
    lax.fori_loop(0, count + skew(count - 1), step, 0)

    for d in range(1, count):
        from_peer(d, hmine, hgot, send_h, recv_h).wait_recv()
    summed = hgot[0]
    for n in range(1, count):
        summed = summed + hgot[n]
    sum_ref[...] = summed
    own_rows = block(me)[...]
    rows_ref[...] = own_rows
    diff = own_rows - last_ref[...]
    square = jnp.sum(diff * diff, axis=0, keepdims=True)
    square = sum(square[:, n * GROUP : (n + 1) * GROUP] for n in range(wide // GROUP))
    square = jnp.broadcast_to(square, smine.shape)
    weight = weight_ref[0:1, :]
    weighted = diff * weight
    for h in range(2):
        pay[h, 0, :half, :] = weighted[h * half : (h + 1) * half]
        pay[h, 0, half:, :] = jnp.zeros((8, wide), F32)
    pay[0, 0, half:, :GROUP] = (summed - last_heads_ref[...]) * weight[:, :GROUP]

    def swap(h, s):
        bit = s if h == 0 else stages - 1 - s
        return remote(
            pay.at[h, s], dgot.at[h, s], send_d.at[h, s], recv_d.at[h, s], "dp", partner(bit)
        )

    for h in range(2):
        swap(h, 0).start()
    smine[...] = square
    sgot[me] = square
    for d in range(1, count):
        to_peer(d, smine, sgot, send_s, recv_s).start()
    for s in range(stages):
        for h in range(2):
            swap(h, s).wait_recv()
            pay[h, s + 1] = pay[h, s] + dgot[h, s]
            if s + 1 < stages:
                swap(h, s + 1).start()
    for h in range(2):
        fired_ref[h * half : (h + 1) * half, :] = pay[h, stages, :half, :]
    fired_heads_ref[...] = pay[0, stages, half:, :GROUP]
    for d in range(1, count):
        from_peer(d, smine, sgot, send_s, recv_s).wait_recv()
    total = sgot[0]
    for n in range(1, count):
        total = total + sgot[n]
    square_ref[...] = total

    for s in range(stages):
        for h in range(2):
            swap(h, s).wait_send()
    for d in range(1, count):
        to_peer(d, hmine, hgot, send_h, recv_h).wait_send()
        to_peer(d, smine, sgot, send_s, recv_s).wait_send()

    def drain(j, unused):
        @pl.when(j > me)
        def _():
            remote(block(j), got_r.at[j], send_r.at[j], recv_r.at[j], "seq", me + 1).wait_send()

        @pl.when(j < me)
        def _():
            remote(block(j), got_l.at[j], send_l.at[j], recv_l.at[j], "seq", me - 1).wait_send()

        return unused

    lax.fori_loop(0, count, drain, 0)


def local(
    count, replicas, tokens, values, out_grad, w_bc, w_dt, a_log, dt_bias, fire_flags,
    last_bc, last_heads, total_bc, total_heads,
):
    tok = tokens[0]
    x = values[0]
    g = out_grad[0]
    length, inner = x.shape
    heads = a_log.shape[0]
    width = inner // heads
    chunks = inner // LANES
    wide = w_bc.shape[1]
    half = wide // 2
    blocks = length // GROUP
    npairs = blocks * (blocks + 1) // 2
    sds = jax.ShapeDtypeStruct
    whole = lambda a: pl.BlockSpec(a.shape, lambda k: (0,) * len(a.shape))
    chunk2 = pl.BlockSpec((length, LANES), lambda k: (0, k))
    chunk3 = pl.BlockSpec((1, half, LANES), lambda k: (k, 0, 0))
    small = sds((length, heads), F32)
    states = sds((chunks, half, LANES), F32)
    outs = [states, states, sds((chunks, 1, LANES), F32), sds((length, wide), F32)] + [small] * 4
    alog2 = a_log[None]
    bias2 = dt_bias[None]
    wdt = w_dt.T
    pair = pltpu.VMEM((2, length, heads), BF16)
    fresh, entry, decay, proj, cum, rate, sigcum, sig = pl.pallas_call(
        functools.partial(front_kernel, width),
        grid=(chunks,),
        in_specs=[whole(tok), whole(w_bc), whole(wdt), whole(alog2), whole(bias2), chunk2, chunk2],
        out_specs=[chunk3, chunk3, pl.BlockSpec((1, 1, LANES), lambda k: (k, 0, 0))]
        + [whole(o) for o in outs[3:]],
        out_shape=outs,
        scratch_shapes=[pair, pair],
        name="front",
    )(tok, w_bc, wdt, alog2, bias2, x, g)
    vm = pl.BlockSpec(memory_space=pltpu.VMEM)
    buf = pltpu.VMEM((chunks, half, LANES), F32)
    sem = pltpu.SemaphoreType.DMA((chunks,))
    square_tiles = pltpu.VMEM((npairs, GROUP, GROUP), F32)
    head_rows = pltpu.VMEM((heads, GROUP), F32)
    d_projected, grad_heads = pl.pallas_call(
        functools.partial(chain_kernel, count, width),
        in_specs=[vm] * 10,
        out_specs=[vm, vm],
        out_shape=[sds((length, wide), BF16), sds((8, GROUP), F32)],
        scratch_shapes=[
            buf, buf, buf, buf, pair, pair,
            pltpu.VMEM((length, heads), F32),
            pltpu.VMEM((length, heads), F32),
            pltpu.VMEM((8, heads), F32),
            pltpu.VMEM((length, wide), F32),
            pltpu.VMEM((5, length, heads), BF16),
            pltpu.VMEM((4, heads, length), F32),
            square_tiles, square_tiles, head_rows, head_rows,
            sem, sem, sem, sem,
        ],
        compiler_params=pltpu.CompilerParams(
            collective_id=0, has_side_effects=True, vmem_limit_bytes=56 * 1024 * 1024
        ),
        name="chain",
    )(decay, fresh, entry, x, g, proj, cum, rate, sigcum, sig)
    own_last = last_bc[0]
    rows = own_last.shape[0]
    stages = replicas.bit_length() - 1
    tile = lambda a: jnp.pad(a, ((0, 8 - a.shape[0]), (0, GROUP - a.shape[1])))
    weight = jnp.broadcast_to(fire_flags[0].astype(F32), (8, wide))
    dma = pltpu.SemaphoreType.DMA
    own_rows, fired_bc, summed, fired, square = pl.pallas_call(
        functools.partial(tail_kernel, count, replicas),
        in_specs=[vm] * 6,
        out_specs=[vm] * 5,
        out_shape=[sds((rows, wide), F32)] * 2 + [sds((8, GROUP), F32)] * 3,
        scratch_shapes=[
            pltpu.VMEM((rows * count, wide), F32),
            pltpu.VMEM((count, rows, wide), F32),
            pltpu.VMEM((count, rows, wide), F32),
            pltpu.VMEM((2, stages + 1, rows // 2 + 8, wide), F32),
            pltpu.VMEM((2, stages, rows // 2 + 8, wide), F32),
            pltpu.VMEM((count, 8, GROUP), F32),
            pltpu.VMEM((8, GROUP), F32),
            pltpu.VMEM((count, 8, GROUP), F32),
            pltpu.VMEM((8, GROUP), F32),
        ]
        + [dma((count,))] * 4 + [dma((2, stages))] * 2 + [dma((count,))] * 4,
        compiler_params=pltpu.CompilerParams(
            collective_id=1, has_side_effects=True, vmem_limit_bytes=48 * 1024 * 1024
        ),
        name="tail",
    )(tok, d_projected, grad_heads, own_last, tile(last_heads[0]), weight)
    summed_heads = summed[:2, :heads]
    diff_heads = summed_heads - last_heads[0]
    trigger = jnp.sqrt(jnp.sum(square[0]) + jnp.sum(diff_heads * diff_heads) + 1e-06)
    new_total_bc = total_bc + fired_bc
    new_total_heads = total_heads + fired[:2, :heads]
    new_last_bc = jnp.where(fire_flags[0] > 0, own_rows, own_last)[None]
    new_last_heads = jnp.where(fire_flags[0] > 0, summed_heads, last_heads[0])[None]
    return (new_total_bc, new_total_heads, new_last_bc, new_last_heads, trigger.reshape(1))


def solution(mesh):
    in_specs = (
        P("dp", "seq", None), P("dp", "seq", None), P("dp", "seq", None), P(), P(), P(), P(),
        P("dp"), P("dp", "seq", None), P("dp", None, None), P("seq", None), P(),
    )
    out_specs = (P("seq", None), P(), P("dp", "seq", None), P("dp", None, None), P("dp"))
    return jax.shard_map(
        functools.partial(local, mesh.shape["seq"], mesh.shape["dp"]), mesh=mesh, in_specs=in_specs,
        out_specs=out_specs, check_vma=False,
    )
```

```python
import functools

import jax
import jax.numpy as jnp
from jax import lax
from jax.experimental import pallas as pl
from jax.experimental.pallas import tpu as pltpu
from jax.sharding import PartitionSpec as P

GROUP = 128
LANES = 256
F32 = jnp.float32
BF16 = jnp.bfloat16
HIGHEST = lax.Precision.HIGHEST
MM = (((1,), (0,)), ((), ()))
NT = (((1,), (1,)), ((), ()))
TN = (((0,), (0,)), ((), ()))


def mm(a, b, dims=MM):
    return lax.dot_general(a, b, dims, preferred_element_type=F32)


def exact(a, b, dims=MM):
    return lax.dot_general(a, b, dims, precision=HIGHEST, preferred_element_type=F32)


def halves(x):
    hi = x.astype(BF16)
    return hi, (x - hi.astype(F32)).astype(BF16)


def mm3(a, b, dims=MM):
    return mm(a[0], b[0], dims) + (mm(a[0], b[1], dims) + mm(a[1], b[0], dims))


def spread(heads, lanes, per_head, first, copies):
    row = lax.broadcasted_iota(jnp.int32, (copies * heads, lanes), 0)
    want = first + lax.broadcasted_iota(jnp.int32, (copies * heads, lanes), 1) // per_head
    hit = row == want
    for n in range(1, copies):
        hit = hit | (row == want + n * heads)
    return hit.astype(F32).astype(BF16)


def stacked(x, copies):
    parts = []
    for n in range(copies):
        part = x.astype(BF16)
        parts.append(part.astype(F32))
        x = x - parts[-1]
    return jnp.concatenate(parts, axis=1).astype(BF16)


def gathers(heads, lanes, per_head, first):
    lane = lax.broadcasted_iota(jnp.int32, (lanes, heads), 0)
    row = lax.broadcasted_iota(jnp.int32, (lanes, heads), 1)
    return (row == first + lane // per_head).astype(F32).astype(BF16)


def front_kernel(
    width, tok_ref, wbc_ref, wdt_ref, alog_ref, bias_ref, x_ref, g_ref,
    fresh_ref, entry_ref, decay_ref, proj_ref, cum_ref, rate_ref, sigcum_ref, sig_ref, w2, flipped,
):
    k = pl.program_id(0)
    length, heads = cum_ref.shape
    half = proj_ref.shape[1] // 2

    @pl.when(k == 0)
    def _():
        tok = tok_ref[...]
        proj = mm(tok, wbc_ref[...])
        proj_ref[...] = proj
        hi, lo = halves(proj.T)
        flipped[0] = hi
        flipped[1] = lo
        z = mm(tok, wdt_ref[...], NT) + bias_ref[...]
        tail = jnp.exp(-jnp.abs(z))
        rate = jnp.maximum(z, 0.0) + jnp.log1p(tail)
        sig = jnp.where(z >= 0, 1.0, tail) / (1.0 + tail)
        speed = jnp.exp(alog_ref[...])
        tri = (
            lax.broadcasted_iota(jnp.int32, (length, length), 0)
            >= lax.broadcasted_iota(jnp.int32, (length, length), 1)
        ).astype(F32)
        cum = exact(tri, -rate * speed)
        cum_ref[...] = cum
        rate_ref[...] = rate
        sig_ref[...] = sig
        sigcum_ref[...] = exact(tri, -sig * speed)
        w2[0] = stacked(jnp.exp(cum), 2)
        w2[1] = stacked(jnp.exp(cum[length - 1 :] - cum) * rate, 2)

    lanes = x_ref.shape[1]
    hot = spread(heads, lanes, width, k * (lanes // width), 2)
    grow = mm(w2[0], hot)
    fade = mm(w2[1], hot)
    decay_ref[0] = grow[length - 1 :]
    b = (flipped[0, :half, :], flipped[1, :half, :])
    c = (flipped[0, half:, :], flipped[1, half:, :])
    fresh_ref[0] = mm3(b, halves(fade * x_ref[...].astype(F32)))
    entry_ref[0] = mm3(c, halves(grow * g_ref[...].astype(F32)))


def chain_kernel(
    count, width, decay_ref, fresh_ref, entry_ref, x_ref, g_ref,
    proj_ref, cum_ref, rate_ref, sigcum_ref, sig_ref, out_ref, heads_ref,
    got_f, got_b, out_f, out_b, w2, bc2, he, hf, gacc, acc, cum3, sig2, rows, score, dscore,
    ra_ref, rb_ref, send_f, recv_f, send_b, recv_b,
):
    me = lax.axis_index("seq")
    chunks, half, lanes = fresh_ref.shape
    length, heads = cum_ref.shape
    blocks = length // GROUP
    pairs = [(i, j) for i in range(blocks) for j in range(i + 1)]
    group = lanes // width
    right = lax.rem(me + 1, count)
    left = lax.rem(me + count - 1, count)
    barrier = pltpu.get_barrier_semaphore()
    for peer in (left, right):
        pl.semaphore_signal(
            barrier, inc=1, device_id={"seq": peer}, device_id_type=pl.DeviceIdType.MESH
        )

    proj = proj_ref[...]
    b, c = proj[:, :half], proj[:, half:]
    cum = cum_ref[...]
    w2[0] = stacked(jnp.exp(cum), 2)
    w2[1] = stacked(jnp.exp(cum[length - 1 :] - cum) * rate_ref[...], 2)
    bc2[0] = stacked(b, 2)
    bc2[1] = stacked(c, 2)
    cum3[...] = stacked(cum, 3)
    sig2[...] = stacked(sigcum_ref[...], 2)
    for n, w in enumerate((cum_ref, rate_ref, sigcum_ref, sig_ref)):
        rows[n] = w[...].T
    for n, (i, j) in enumerate(pairs):
        score[n] = exact(c[i * GROUP : (i + 1) * GROUP], b[j * GROUP : (j + 1) * GROUP], NT)
    dscore[...] = jnp.zeros_like(dscore)
    he[...] = jnp.zeros_like(he)
    hf[...] = jnp.zeros_like(hf)
    gacc[...] = jnp.zeros_like(gacc)
    acc[...] = jnp.zeros_like(acc)
    pl.semaphore_wait(barrier, 2)

    def forward(k):
        return remote(out_f.at[k], got_f.at[k], send_f.at[k], recv_f.at[k], "seq", right)

    def backward(k):
        return remote(out_b.at[k], got_b.at[k], send_b.at[k], recv_b.at[k], "seq", left)

    def columns(k):
        return pl.ds(pl.multiple_of(k * lanes, lanes), lanes)

    def inner_terms(k):
        xs = x_ref[:, columns(k)]
        gs = g_ref[:, columns(k)]
        causal = lax.broadcasted_iota(jnp.int32, (GROUP, GROUP), 0) >= lax.broadcasted_iota(
            jnp.int32, (GROUP, GROUP), 1
        )
        lane_head = lax.broadcasted_iota(jnp.int32, (GROUP, lanes), 1) // width
        span = max(GROUP, width)
        for one in range(group):
            head = k * group + one
            pick = spread(heads, GROUP, GROUP, head, 3)
            cum_col = mm(cum3[...], pick)
            sig_col = mm(sig2[...], pick[: 2 * heads])
            at = pl.ds(head, 1)
            cum_row, rate_row, sc_row, sig_row = (rows[n, at, :] for n in range(4))
            ra = jnp.zeros((1, GROUP), F32)
            rb = jnp.zeros((1, GROUP), F32)
            low = (one * width) // GROUP * GROUP
            own = jnp.where(lane_head[:, low : low + span] == one, 1.0, 0.0).astype(BF16)
            for n, (i, j) in enumerate(pairs):
                ti = slice(i * GROUP, (i + 1) * GROUP)
                sj = slice(j * GROUP, (j + 1) * GROUP)
                gap = cum_col[ti] - cum_row[:, sj]
                if i == j:
                    gap = jnp.where(causal, gap, -1e30)
                inner = mm(gs[ti, low : low + span] * own, xs[sj, low : low + span], NT)
                mixed = jnp.exp(gap) * inner
                dscore[n] += mixed * rate_row[:, sj]
                q = score[n] * mixed
                c0 = jnp.sum(q, axis=0, keepdims=True)
                if i == j:
                    gap = jnp.where(causal, gap, 0.0)
                c1 = jnp.sum(q * gap, axis=0, keepdims=True)
                c2 = jnp.sum(q * sig_col[ti], axis=0, keepdims=True)
                ra += rate_row[:, sj] * c1
                rb += rate_row[:, sj] * (c2 - sc_row[:, sj] * c0) + sig_row[:, sj] * c0
            ra_ref[at, :] = ra
            rb_ref[at, :] = rb

    def outer_terms(k):
        hot = spread(heads, lanes, width, k * group, 2)
        cold = gathers(heads, lanes, width, k * group)
        xf = x_ref[:, columns(k)].astype(F32)
        gf = g_ref[:, columns(k)].astype(F32)
        state = got_f[k]
        back = got_b[k]
        state2 = halves(state)
        back2 = halves(back)
        grow = mm(w2[0], hot)
        fade = mm(w2[1], hot)

        def read(n, part):
            twice = jnp.concatenate([part[0], part[0]], axis=0)
            return mm(bc2[n], twice) + mm(bc2[n, :, :half], part[1])

        hi, lo = halves(gf * read(1, state2))
        he[...] += mm(hi, cold) + mm(lo, cold)
        hi, lo = halves(xf * read(0, back2))
        hf[...] += mm(hi, cold) + mm(lo, cold)
        acc[:, half:] += mm3(halves(grow * gf), state2, NT)
        acc[:, :half] += mm3(halves(fade * xf), back2, NT)
        both = jnp.broadcast_to(jnp.sum(state * back, axis=0, keepdims=True), (8, lanes))
        hi, lo = halves(both)
        gacc[...] += mm(hi, cold) + mm(lo, cold)

    lead = skew(count - 1)
    each = pl.cdiv(chunks, lead)
    ahead = skew(me)
    behind = skew(count - 1 - me)

    def step(tau, unused):
        k = tau - ahead

        @pl.when((k >= 0) & (k < chunks))
        def _():
            @pl.when(me == 0)
            def _():
                got_f[k] = jnp.zeros((half, lanes), F32)
                out_f[k] = fresh_ref[k]

            @pl.when(me > 0)
            def _():
                forward(k).wait_recv()

                @pl.when(me < count - 1)
                def _():
                    out_f[k] = decay_ref[k] * got_f[k] + fresh_ref[k]

            @pl.when(me < count - 1)
            def _():
                forward(k).start()

        j = tau - behind

        @pl.when((j >= 0) & (j < chunks))
        def _():
            @pl.when(me == count - 1)
            def _():
                got_b[j] = jnp.zeros((half, lanes), F32)
                out_b[j] = entry_ref[j]

            @pl.when(me < count - 1)
            def _():
                backward(j).wait_recv()

                @pl.when(me > 0)
                def _():
                    out_b[j] = decay_ref[j] * got_b[j] + entry_ref[j]

            @pl.when(me > 0)
            def _():
                backward(j).start()

        @pl.when(tau < lead)
        def _():
            for n in range(each):
                item = tau * each + n

                @pl.when(item < chunks)
                def _():
                    inner_terms(item)

        @pl.when(tau >= lead)
        def _():
            outer_terms(tau - lead)

        return unused

    lax.fori_loop(0, chunks + lead, step, 0)

    for n, (i, j) in enumerate(pairs):
        ti = slice(i * GROUP, (i + 1) * GROUP)
        sj = slice(j * GROUP, (j + 1) * GROUP)
        d = halves(dscore[n])
        acc[ti, half:] += mm3(d, halves(b[sj]))
        acc[sj, :half] += mm3(d, halves(c[ti]), TN)
    out_ref[...] = acc[...].astype(BF16)
    sigcum = sigcum_ref[...]
    last = cum[length - 1 :]
    sig_last = sigcum[length - 1 :]
    e = jnp.exp(cum) * he[...]
    f0 = jnp.exp(last - cum) * hf[...]
    f = f0 * rate_ref[...]
    link = jnp.exp(last) * gacc[0:1, :]
    ga = jnp.sum(e * cum + f * (last - cum), axis=0, keepdims=True) + link * last
    gb = (
        jnp.sum(e * sigcum + f * (sig_last - sigcum) + f0 * sig_ref[...], axis=0, keepdims=True)
        + link * sig_last
    )
    heads_ref[...] = jnp.zeros_like(heads_ref)
    heads_ref[0:1, :heads] = ga + jnp.sum(ra_ref[...].T, axis=0, keepdims=True)
    heads_ref[1:2, :heads] = gb + jnp.sum(rb_ref[...].T, axis=0, keepdims=True)

    def drain(k, unused):
        @pl.when(me < count - 1)
        def _():
            forward(k).wait_send()

        @pl.when(me > 0)
        def _():
            backward(k).wait_send()

        return unused

    lax.fori_loop(0, chunks, drain, 0)


def remote(src, dst, send, recv, axis, peer):
    return pltpu.make_async_remote_copy(
        src_ref=src, dst_ref=dst, send_sem=send, recv_sem=recv, device_id={axis: peer},
        device_id_type=pl.DeviceIdType.MESH,
    )


def skew(place):
    return 3 * (place // 2) + place % 2


def tail_kernel(
    count, replicas, tok_ref, dproj_ref, heads_ref, last_ref, last_heads_ref, weight_ref,
    rows_ref, fired_ref, sum_ref, fired_heads_ref, square_ref,
    own, got_r, got_l, pay, dgot, hgot, hmine, sgot, smine,
    send_r, recv_r, send_l, recv_l, send_d, recv_d, send_h, recv_h, send_s, recv_s,
):
    me = lax.axis_index("seq")
    mine = lax.axis_index("dp")
    rows = last_ref.shape[0]
    half = rows // 2
    wide = last_ref.shape[1]
    stages = replicas.bit_length() - 1
    parts = got_r.shape[0] // count
    piece = rows // parts

    def partner(bit):
        size = 2**bit
        return mine + size * (1 - 2 * (mine // size % 2))

    barrier = pltpu.get_barrier_semaphore()
    for d in range(1, count):
        pl.semaphore_signal(
            barrier, inc=1, device_id={"seq": lax.rem(me + d, count)},
            device_id_type=pl.DeviceIdType.MESH,
        )
    for bit in range(stages):
        pl.semaphore_signal(
            barrier, inc=1, device_id={"dp": partner(bit)}, device_id_type=pl.DeviceIdType.MESH
        )

    hmine[...] = heads_ref[...]
    hgot[me] = heads_ref[...]
    tok_rows = tok_ref.shape[1] // wide
    dproj = dproj_ref[...]
    for n in range(tok_rows):
        own[n * wide : (n + 1) * wide, :] = mm(tok_ref[:, n * wide : (n + 1) * wide], dproj, TN)
    pl.semaphore_wait(barrier, count - 1 + stages)

    def to_peer(d, src, got, send, recv):
        return remote(
            src, got.at[me], send.at[d], recv.at[me], "seq", lax.rem(me + d, count)
        )

    def from_peer(d, src, got, send, recv):
        place = lax.rem(me + d, count)
        return remote(src, got.at[place], send.at[d], recv.at[place], "seq", place)

    def block(j):
        return own.at[pl.ds(pl.multiple_of(j * piece, 8), piece)]

    def step(tau, unused):
        t = tau - skew(me)
        j = count * parts - 1 - t

        @pl.when((t >= 0) & (j >= me * parts))
        def _():
            ref = block(j)

            @pl.when(me > 0)
            def _():
                remote(ref, got_r.at[j], send_r.at[j], recv_r.at[j], "seq", me - 1).wait_recv()
                ref[...] += got_r[j]

            @pl.when(j >= (me + 1) * parts)
            def _():
                remote(ref, got_r.at[j], send_r.at[j], recv_r.at[j], "seq", me + 1).start()

        u = tau - skew(count - 1 - me)

        @pl.when((u >= 0) & (u < (me + 1) * parts))
        def _():
            ref = block(u)

            @pl.when(me < count - 1)
            def _():
                remote(ref, got_l.at[u], send_l.at[u], recv_l.at[u], "seq", me + 1).wait_recv()
                ref[...] += got_l[u]

            @pl.when(u < me * parts)
            def _():
                remote(ref, got_l.at[u], send_l.at[u], recv_l.at[u], "seq", me - 1).start()

        return unused

    for d in range(1, count):
        to_peer(d, hmine, hgot, send_h, recv_h).start()
    lax.fori_loop(0, count * parts + skew(count - 1), step, 0)

    for d in range(1, count):
        from_peer(d, hmine, hgot, send_h, recv_h).wait_recv()
    summed = hgot[0]
    for n in range(1, count):
        summed = summed + hgot[n]
    sum_ref[...] = summed
    own_rows = own[pl.ds(pl.multiple_of(me * rows, 8), rows), :]
    rows_ref[...] = own_rows
    diff = own_rows - last_ref[...]
    square = jnp.sum(diff * diff, axis=0, keepdims=True)
    square = sum(square[:, n * GROUP : (n + 1) * GROUP] for n in range(wide // GROUP))
    square = jnp.broadcast_to(square, smine.shape)
    weight = weight_ref[0:1, :]
    weighted = diff * weight
    for h in range(2):
        pay[h, 0, :half, :] = weighted[h * half : (h + 1) * half]
        pay[h, 0, half:, :] = jnp.zeros((8, wide), F32)
    pay[0, 0, half:, :GROUP] = (summed - last_heads_ref[...]) * weight[:, :GROUP]

    def swap(h, s):
        bit = s if h == 0 else stages - 1 - s
        return remote(
            pay.at[h, s], dgot.at[h, s], send_d.at[h, s], recv_d.at[h, s], "dp", partner(bit)
        )

    for h in range(2):
        swap(h, 0).start()
    smine[...] = square
    sgot[me] = square
    for d in range(1, count):
        to_peer(d, smine, sgot, send_s, recv_s).start()
    for s in range(stages):
        for h in range(2):
            swap(h, s).wait_recv()
            pay[h, s + 1] = pay[h, s] + dgot[h, s]
            if s + 1 < stages:
                swap(h, s + 1).start()
    for h in range(2):
        fired_ref[h * half : (h + 1) * half, :] = pay[h, stages, :half, :]
    fired_heads_ref[...] = pay[0, stages, half:, :GROUP]
    for d in range(1, count):
        from_peer(d, smine, sgot, send_s, recv_s).wait_recv()
    total = sgot[0]
    for n in range(1, count):
        total = total + sgot[n]
    off = summed - last_heads_ref[...]
    line = total[0:1, :] + jnp.sum(off * off, axis=0, keepdims=True)
    line = jnp.broadcast_to(jnp.sum(line, axis=1, keepdims=True), square_ref.shape)
    square_ref[...] = jnp.sqrt(line + 1e-06)

    for s in range(stages):
        for h in range(2):
            swap(h, s).wait_send()
    for d in range(1, count):
        to_peer(d, hmine, hgot, send_h, recv_h).wait_send()
        to_peer(d, smine, sgot, send_s, recv_s).wait_send()

    def drain(j, unused):
        @pl.when(j >= (me + 1) * parts)
        def _():
            remote(block(j), got_r.at[j], send_r.at[j], recv_r.at[j], "seq", me + 1).wait_send()

        @pl.when(j < me * parts)
        def _():
            remote(block(j), got_l.at[j], send_l.at[j], recv_l.at[j], "seq", me - 1).wait_send()

        return unused

    lax.fori_loop(0, count * parts, drain, 0)


def local(
    count, replicas, tokens, values, out_grad, w_bc, w_dt, a_log, dt_bias, fire_flags,
    last_bc, last_heads, total_bc, total_heads,
):
    tok = tokens[0]
    x = values[0]
    g = out_grad[0]
    length, inner = x.shape
    heads = a_log.shape[0]
    width = inner // heads
    chunks = inner // LANES
    wide = w_bc.shape[1]
    half = wide // 2
    blocks = length // GROUP
    npairs = blocks * (blocks + 1) // 2
    sds = jax.ShapeDtypeStruct
    whole = lambda a: pl.BlockSpec(a.shape, lambda k: (0,) * len(a.shape))
    chunk2 = pl.BlockSpec((length, LANES), lambda k: (0, k))
    chunk3 = pl.BlockSpec((1, half, LANES), lambda k: (k, 0, 0))
    small = sds((length, heads), F32)
    states = sds((chunks, half, LANES), F32)
    outs = [states, states, sds((chunks, 1, LANES), F32), sds((length, wide), F32)] + [small] * 4
    alog2 = a_log[None]
    bias2 = dt_bias[None]
    wdt = w_dt.T
    pair = pltpu.VMEM((2, length, 2 * heads), BF16)
    fresh, entry, decay, proj, cum, rate, sigcum, sig = pl.pallas_call(
        functools.partial(front_kernel, width),
        grid=(chunks,),
        in_specs=[whole(tok), whole(w_bc), whole(wdt), whole(alog2), whole(bias2), chunk2, chunk2],
        out_specs=[chunk3, chunk3, pl.BlockSpec((1, 1, LANES), lambda k: (k, 0, 0))]
        + [whole(o) for o in outs[3:]],
        out_shape=outs,
        scratch_shapes=[pair, pltpu.VMEM((2, wide, length), BF16)],
        name="front",
    )(tok, w_bc, wdt, alog2, bias2, x, g)
    vm = pl.BlockSpec(memory_space=pltpu.VMEM)
    buf = pltpu.VMEM((chunks, half, LANES), F32)
    sem = pltpu.SemaphoreType.DMA((chunks,))
    square_tiles = pltpu.VMEM((npairs, GROUP, GROUP), F32)
    head_rows = pltpu.VMEM((heads, GROUP), F32)
    d_projected, grad_heads = pl.pallas_call(
        functools.partial(chain_kernel, count, width),
        in_specs=[vm] * 10,
        out_specs=[vm, vm],
        out_shape=[sds((length, wide), BF16), sds((8, GROUP), F32)],
        scratch_shapes=[
            buf, buf, buf, buf, pair, pltpu.VMEM((2, length, wide), BF16),
            pltpu.VMEM((length, heads), F32),
            pltpu.VMEM((length, heads), F32),
            pltpu.VMEM((8, heads), F32),
            pltpu.VMEM((length, wide), F32),
            pltpu.VMEM((length, 3 * heads), BF16),
            pltpu.VMEM((length, 2 * heads), BF16),
            pltpu.VMEM((4, heads, length), F32),
            square_tiles, square_tiles, head_rows, head_rows,
            sem, sem, sem, sem,
        ],
        compiler_params=pltpu.CompilerParams(
            collective_id=0, has_side_effects=True, vmem_limit_bytes=56 * 1024 * 1024
        ),
        name="chain",
    )(decay, fresh, entry, x, g, proj, cum, rate, sigcum, sig)
    own_last = last_bc[0]
    rows = own_last.shape[0]
    stages = replicas.bit_length() - 1
    tile = lambda a: jnp.pad(a, ((0, 8 - a.shape[0]), (0, GROUP - a.shape[1])))
    weight = jnp.broadcast_to(fire_flags[0].astype(F32), (8, wide))
    dma = pltpu.SemaphoreType.DMA
    parts = 2 if rows % 16 == 0 else 1
    own_rows, fired_bc, summed, fired, square = pl.pallas_call(
        functools.partial(tail_kernel, count, replicas),
        in_specs=[vm] * 6,
        out_specs=[vm] * 5,
        out_shape=[sds((rows, wide), F32)] * 2 + [sds((8, GROUP), F32)] * 3,
        scratch_shapes=[
            pltpu.VMEM((rows * count, wide), F32),
            pltpu.VMEM((count * parts, rows // parts, wide), F32),
            pltpu.VMEM((count * parts, rows // parts, wide), F32),
            pltpu.VMEM((2, stages + 1, rows // 2 + 8, wide), F32),
            pltpu.VMEM((2, stages, rows // 2 + 8, wide), F32),
            pltpu.VMEM((count, 8, GROUP), F32),
            pltpu.VMEM((8, GROUP), F32),
            pltpu.VMEM((count, 8, GROUP), F32),
            pltpu.VMEM((8, GROUP), F32),
        ]
        + [dma((count * parts,))] * 4 + [dma((2, stages))] * 2 + [dma((count,))] * 4,
        compiler_params=pltpu.CompilerParams(
            collective_id=1, has_side_effects=True, vmem_limit_bytes=48 * 1024 * 1024
        ),
        name="tail",
    )(tok, d_projected, grad_heads, own_last, tile(last_heads[0]), weight)
    summed_heads = summed[:2, :heads]
    new_total_bc = total_bc + fired_bc
    new_total_heads = total_heads + fired[:2, :heads]
    new_last_bc = jnp.where(fire_flags[0] > 0, own_rows, own_last)[None]
    new_last_heads = jnp.where(fire_flags[0] > 0, summed_heads, last_heads[0])[None]
    return (new_total_bc, new_total_heads, new_last_bc, new_last_heads, square[0, :1])


def solution(mesh):
    in_specs = (
        P("dp", "seq", None), P("dp", "seq", None), P("dp", "seq", None), P(), P(), P(), P(),
        P("dp"), P("dp", "seq", None), P("dp", None, None), P("seq", None), P(),
    )
    out_specs = (P("seq", None), P(), P("dp", "seq", None), P("dp", None, None), P("dp"))
    return jax.shard_map(
        functools.partial(local, mesh.shape["seq"], mesh.shape["dp"]), mesh=mesh, in_specs=in_specs,
        out_specs=out_specs, check_vma=False,
    )
```

```python
import functools

import jax
import jax.numpy as jnp
from jax import lax
from jax.experimental import pallas as pl
from jax.experimental.pallas import tpu as pltpu
from jax.sharding import PartitionSpec as P

GROUP = 128
LANES = 256
F32 = jnp.float32
BF16 = jnp.bfloat16
HIGHEST = lax.Precision.HIGHEST
MM = (((1,), (0,)), ((), ()))
NT = (((1,), (1,)), ((), ()))
TN = (((0,), (0,)), ((), ()))


def mm(a, b, dims=MM):
    return lax.dot_general(a, b, dims, preferred_element_type=F32)


def exact(a, b, dims=MM):
    return lax.dot_general(a, b, dims, precision=HIGHEST, preferred_element_type=F32)


def halves(x):
    hi = x.astype(BF16)
    return hi, (x - hi.astype(F32)).astype(BF16)


def mm3(a, b, dims=MM):
    return mm(a[0], b[0], dims) + (mm(a[0], b[1], dims) + mm(a[1], b[0], dims))


def spread(heads, lanes, per_head, first, copies):
    row = lax.broadcasted_iota(jnp.int32, (copies * heads, lanes), 0)
    want = first + lax.broadcasted_iota(jnp.int32, (copies * heads, lanes), 1) // per_head
    hit = row == want
    for n in range(1, copies):
        hit = hit | (row == want + n * heads)
    return hit.astype(F32).astype(BF16)


def stacked(x, copies):
    parts = []
    for n in range(copies):
        part = x.astype(BF16)
        parts.append(part.astype(F32))
        x = x - parts[-1]
    return jnp.concatenate(parts, axis=1).astype(BF16)


def gathers(heads, lanes, per_head, first):
    lane = lax.broadcasted_iota(jnp.int32, (lanes, heads), 0)
    row = lax.broadcasted_iota(jnp.int32, (lanes, heads), 1)
    return (row == first + lane // per_head).astype(F32).astype(BF16)


def front_kernel(
    width, tok_ref, wbc_ref, wdt_ref, alog_ref, bias_ref, x_ref, g_ref,
    fresh_ref, entry_ref, decay_ref, proj_ref, cum_ref, rate_ref, sigcum_ref, sig_ref, w2, flipped,
):
    k = pl.program_id(0)
    length, heads = cum_ref.shape

    @pl.when(k == 0)
    def _():
        tok = tok_ref[...]
        proj = mm(tok, wbc_ref[...])
        proj_ref[...] = proj
        hi, lo = halves(proj.T)
        flipped[0] = hi
        flipped[1] = lo
        z = mm(tok, wdt_ref[...], NT) + bias_ref[...]
        tail = jnp.exp(-jnp.abs(z))
        rate = jnp.maximum(z, 0.0) + jnp.log1p(tail)
        sig = jnp.where(z >= 0, 1.0, tail) / (1.0 + tail)
        speed = jnp.exp(alog_ref[...])
        tri = (
            lax.broadcasted_iota(jnp.int32, (length, length), 0)
            >= lax.broadcasted_iota(jnp.int32, (length, length), 1)
        ).astype(F32)
        cum = exact(tri, -rate * speed)
        cum_ref[...] = cum
        rate_ref[...] = rate
        sig_ref[...] = sig
        sigcum_ref[...] = exact(tri, -sig * speed)
        w2[0] = stacked(jnp.exp(cum), 2)
        w2[1] = stacked(jnp.exp(cum[length - 1 :] - cum) * rate, 2)

    per, half, lanes = fresh_ref.shape
    b = (flipped[0, :half, :], flipped[1, :half, :])
    c = (flipped[0, half:, :], flipped[1, half:, :])
    for n in range(per):
        hot = spread(heads, lanes, width, (k * per + n) * (lanes // width), 2)
        grow = mm(w2[0], hot)
        fade = mm(w2[1], hot)
        decay_ref[n] = grow[length - 1 :]
        at = slice(n * lanes, (n + 1) * lanes)
        fresh_ref[n] = mm3(b, halves(fade * x_ref[:, at].astype(F32)))
        entry_ref[n] = mm3(c, halves(grow * g_ref[:, at].astype(F32)))


def chain_kernel(
    count, width, decay_ref, fresh_ref, entry_ref, x_ref, g_ref,
    proj_ref, cum_ref, rate_ref, sigcum_ref, sig_ref, out_ref, heads_ref,
    got_f, got_b, out_f, out_b, w2, bc2, he, hf, gacc, acc, cum3, sig2, rows, score, dscore,
    ra_ref, rb_ref, send_f, recv_f, send_b, recv_b,
):
    me = lax.axis_index("seq")
    chunks, half, lanes = fresh_ref.shape
    length, heads = cum_ref.shape
    blocks = length // GROUP
    pairs = [(i, j) for i in range(blocks) for j in range(i + 1)]
    group = lanes // width
    right = lax.rem(me + 1, count)
    left = lax.rem(me + count - 1, count)
    barrier = pltpu.get_barrier_semaphore()
    for peer in (left, right):
        pl.semaphore_signal(
            barrier, inc=1, device_id={"seq": peer}, device_id_type=pl.DeviceIdType.MESH
        )

    proj = proj_ref[...]
    b, c = proj[:, :half], proj[:, half:]
    cum = cum_ref[...]
    w2[0] = stacked(jnp.exp(cum), 2)
    w2[1] = stacked(jnp.exp(cum[length - 1 :] - cum) * rate_ref[...], 2)
    bc2[0] = stacked(b, 2)
    bc2[1] = stacked(c, 2)
    cum3[...] = stacked(cum, 3)
    sig2[...] = stacked(sigcum_ref[...], 2)
    for n, w in enumerate((cum_ref, rate_ref, sigcum_ref, sig_ref)):
        rows[n] = w[...].T
    for n, (i, j) in enumerate(pairs):
        score[n] = exact(c[i * GROUP : (i + 1) * GROUP], b[j * GROUP : (j + 1) * GROUP], NT)
    dscore[...] = jnp.zeros_like(dscore)
    he[...] = jnp.zeros_like(he)
    hf[...] = jnp.zeros_like(hf)
    gacc[...] = jnp.zeros_like(gacc)
    acc[...] = jnp.zeros_like(acc)
    pl.semaphore_wait(barrier, 2)

    def forward(k):
        return remote(out_f.at[k], got_f.at[k], send_f.at[k], recv_f.at[k], "seq", right)

    def backward(k):
        return remote(out_b.at[k], got_b.at[k], send_b.at[k], recv_b.at[k], "seq", left)

    def columns(k):
        return pl.ds(pl.multiple_of(k * lanes, lanes), lanes)

    def inner_terms(k):
        xs = x_ref[:, columns(k)]
        gs = g_ref[:, columns(k)]
        causal = lax.broadcasted_iota(jnp.int32, (GROUP, GROUP), 0) >= lax.broadcasted_iota(
            jnp.int32, (GROUP, GROUP), 1
        )
        lane_head = lax.broadcasted_iota(jnp.int32, (GROUP, lanes), 1) // width
        span = max(GROUP, width)
        for one in range(group):
            head = k * group + one
            pick = spread(heads, GROUP, GROUP, head, 3)
            cum_col = mm(cum3[...], pick)
            sig_col = mm(sig2[...], pick[: 2 * heads])
            at = pl.ds(head, 1)
            cum_row, rate_row, sc_row, sig_row = (rows[n, at, :] for n in range(4))
            ra = jnp.zeros((1, GROUP), F32)
            rb = jnp.zeros((1, GROUP), F32)
            low = (one * width) // GROUP * GROUP
            own = jnp.where(lane_head[:, low : low + span] == one, 1.0, 0.0).astype(BF16)
            for n, (i, j) in enumerate(pairs):
                ti = slice(i * GROUP, (i + 1) * GROUP)
                sj = slice(j * GROUP, (j + 1) * GROUP)
                gap = cum_col[ti] - cum_row[:, sj]
                if i == j:
                    gap = jnp.where(causal, gap, -1e30)
                inner = mm(gs[ti, low : low + span] * own, xs[sj, low : low + span], NT)
                mixed = jnp.exp(gap) * inner
                dscore[n] += mixed * rate_row[:, sj]
                q = score[n] * mixed
                c0 = jnp.sum(q, axis=0, keepdims=True)
                if i == j:
                    gap = jnp.where(causal, gap, 0.0)
                c1 = jnp.sum(q * gap, axis=0, keepdims=True)
                c2 = jnp.sum(q * sig_col[ti], axis=0, keepdims=True)
                ra += rate_row[:, sj] * c1
                rb += rate_row[:, sj] * (c2 - sc_row[:, sj] * c0) + sig_row[:, sj] * c0
            ra_ref[at, :] = ra
            rb_ref[at, :] = rb

    def outer_terms(k):
        hot = spread(heads, lanes, width, k * group, 2)
        cold = gathers(heads, lanes, width, k * group)
        xf = x_ref[:, columns(k)].astype(F32)
        gf = g_ref[:, columns(k)].astype(F32)
        state = got_f[k]
        back = got_b[k]
        state2 = halves(state)
        back2 = halves(back)
        grow = mm(w2[0], hot)
        fade = mm(w2[1], hot)

        def read(n, part):
            twice = jnp.concatenate([part[0], part[0]], axis=0)
            return mm(bc2[n], twice) + mm(bc2[n, :, :half], part[1])

        hi, lo = halves(gf * read(1, state2))
        he[...] += mm(hi, cold) + mm(lo, cold)
        hi, lo = halves(xf * read(0, back2))
        hf[...] += mm(hi, cold) + mm(lo, cold)
        acc[:, half:] += mm3(halves(grow * gf), state2, NT)
        acc[:, :half] += mm3(halves(fade * xf), back2, NT)
        both = jnp.broadcast_to(jnp.sum(state * back, axis=0, keepdims=True), (8, lanes))
        hi, lo = halves(both)
        gacc[...] += mm(hi, cold) + mm(lo, cold)

    lead = skew(count - 1)
    each = pl.cdiv(chunks, lead)
    ahead = skew(me)
    behind = skew(count - 1 - me)

    def step(tau, unused):
        k = tau - ahead

        @pl.when((k >= 0) & (k < chunks))
        def _():
            @pl.when(me == 0)
            def _():
                got_f[k] = jnp.zeros((half, lanes), F32)
                out_f[k] = fresh_ref[k]

            @pl.when(me > 0)
            def _():
                forward(k).wait_recv()

                @pl.when(me < count - 1)
                def _():
                    out_f[k] = decay_ref[k] * got_f[k] + fresh_ref[k]

            @pl.when(me < count - 1)
            def _():
                forward(k).start()

        j = tau - behind

        @pl.when((j >= 0) & (j < chunks))
        def _():
            @pl.when(me == count - 1)
            def _():
                got_b[j] = jnp.zeros((half, lanes), F32)
                out_b[j] = entry_ref[j]

            @pl.when(me < count - 1)
            def _():
                backward(j).wait_recv()

                @pl.when(me > 0)
                def _():
                    out_b[j] = decay_ref[j] * got_b[j] + entry_ref[j]

            @pl.when(me > 0)
            def _():
                backward(j).start()

        @pl.when(tau < lead)
        def _():
            for n in range(each):
                item = tau * each + n

                @pl.when(item < chunks)
                def _():
                    inner_terms(item)

        @pl.when(tau >= lead)
        def _():
            outer_terms(tau - lead)

        return unused

    lax.fori_loop(0, chunks + lead, step, 0)

    for n, (i, j) in enumerate(pairs):
        ti = slice(i * GROUP, (i + 1) * GROUP)
        sj = slice(j * GROUP, (j + 1) * GROUP)
        d = halves(dscore[n])
        acc[ti, half:] += mm3(d, halves(b[sj]))
        acc[sj, :half] += mm3(d, halves(c[ti]), TN)
    out_ref[...] = acc[...].astype(BF16)
    sigcum = sigcum_ref[...]
    last = cum[length - 1 :]
    sig_last = sigcum[length - 1 :]
    e = jnp.exp(cum) * he[...]
    f0 = jnp.exp(last - cum) * hf[...]
    f = f0 * rate_ref[...]
    link = jnp.exp(last) * gacc[0:1, :]
    ga = jnp.sum(e * cum + f * (last - cum), axis=0, keepdims=True) + link * last
    gb = (
        jnp.sum(e * sigcum + f * (sig_last - sigcum) + f0 * sig_ref[...], axis=0, keepdims=True)
        + link * sig_last
    )
    heads_ref[...] = jnp.zeros_like(heads_ref)
    heads_ref[0:1, :heads] = ga + jnp.sum(ra_ref[...].T, axis=0, keepdims=True)
    heads_ref[1:2, :heads] = gb + jnp.sum(rb_ref[...].T, axis=0, keepdims=True)

    def drain(k, unused):
        @pl.when(me < count - 1)
        def _():
            forward(k).wait_send()

        @pl.when(me > 0)
        def _():
            backward(k).wait_send()

        return unused

    lax.fori_loop(0, chunks, drain, 0)


def remote(src, dst, send, recv, axis, peer):
    return pltpu.make_async_remote_copy(
        src_ref=src, dst_ref=dst, send_sem=send, recv_sem=recv, device_id={axis: peer},
        device_id_type=pl.DeviceIdType.MESH,
    )


def skew(place):
    return 3 * (place // 2) + place % 2


def tail_kernel(
    count, replicas, tok_ref, dproj_ref, heads_ref, last_ref, last_heads_ref, weight_ref,
    rows_ref, fired_ref, sum_ref, fired_heads_ref, square_ref,
    own, got_r, got_l, pay, dgot, hgot, hmine, sgot, smine,
    send_r, recv_r, send_l, recv_l, send_d, recv_d, send_h, recv_h, send_s, recv_s,
):
    me = lax.axis_index("seq")
    mine = lax.axis_index("dp")
    rows = last_ref.shape[0]
    half = rows // 2
    wide = last_ref.shape[1]
    stages = replicas.bit_length() - 1
    parts = got_r.shape[0] // count
    piece = rows // parts

    def partner(bit):
        size = 2**bit
        return mine + size * (1 - 2 * (mine // size % 2))

    barrier = pltpu.get_barrier_semaphore()
    for d in range(1, count):
        pl.semaphore_signal(
            barrier, inc=1, device_id={"seq": lax.rem(me + d, count)},
            device_id_type=pl.DeviceIdType.MESH,
        )
    for bit in range(stages):
        pl.semaphore_signal(
            barrier, inc=1, device_id={"dp": partner(bit)}, device_id_type=pl.DeviceIdType.MESH
        )

    hmine[...] = heads_ref[...]
    hgot[me] = heads_ref[...]
    tok_rows = tok_ref.shape[1] // wide
    dproj = dproj_ref[...]
    for n in range(tok_rows):
        own[n * wide : (n + 1) * wide, :] = mm(tok_ref[:, n * wide : (n + 1) * wide], dproj, TN)
    pl.semaphore_wait(barrier, count - 1 + stages)

    def to_peer(d, src, got, send, recv):
        return remote(
            src, got.at[me], send.at[d], recv.at[me], "seq", lax.rem(me + d, count)
        )

    def from_peer(d, src, got, send, recv):
        place = lax.rem(me + d, count)
        return remote(src, got.at[place], send.at[d], recv.at[place], "seq", place)

    def block(j):
        return own.at[pl.ds(pl.multiple_of(j * piece, 8), piece)]

    def step(tau, unused):
        t = tau - skew(me)
        j = count * parts - 1 - t

        @pl.when((t >= 0) & (j >= me * parts))
        def _():
            ref = block(j)

            @pl.when(me > 0)
            def _():
                remote(ref, got_r.at[j], send_r.at[j], recv_r.at[j], "seq", me - 1).wait_recv()
                ref[...] += got_r[j]

            @pl.when(j >= (me + 1) * parts)
            def _():
                remote(ref, got_r.at[j], send_r.at[j], recv_r.at[j], "seq", me + 1).start()

        u = tau - skew(count - 1 - me)

        @pl.when((u >= 0) & (u < (me + 1) * parts))
        def _():
            ref = block(u)

            @pl.when(me < count - 1)
            def _():
                remote(ref, got_l.at[u], send_l.at[u], recv_l.at[u], "seq", me + 1).wait_recv()
                ref[...] += got_l[u]

            @pl.when(u < me * parts)
            def _():
                remote(ref, got_l.at[u], send_l.at[u], recv_l.at[u], "seq", me - 1).start()

        return unused

    for d in range(1, count):
        to_peer(d, hmine, hgot, send_h, recv_h).start()
    lax.fori_loop(0, count * parts + skew(count - 1), step, 0)

    for d in range(1, count):
        from_peer(d, hmine, hgot, send_h, recv_h).wait_recv()
    summed = hgot[0]
    for n in range(1, count):
        summed = summed + hgot[n]
    sum_ref[...] = summed
    own_rows = own[pl.ds(pl.multiple_of(me * rows, 8), rows), :]
    rows_ref[...] = own_rows
    diff = own_rows - last_ref[...]
    square = jnp.sum(diff * diff, axis=0, keepdims=True)
    square = sum(square[:, n * GROUP : (n + 1) * GROUP] for n in range(wide // GROUP))
    square = jnp.broadcast_to(square, smine.shape)
    weight = weight_ref[0:1, :]
    weighted = diff * weight
    for h in range(2):
        pay[h, 0, :half, :] = weighted[h * half : (h + 1) * half]
        pay[h, 0, half:, :] = jnp.zeros((8, wide), F32)
    pay[0, 0, half:, :GROUP] = (summed - last_heads_ref[...]) * weight[:, :GROUP]

    def swap(h, s):
        bit = s if h == 0 else stages - 1 - s
        return remote(
            pay.at[h, s], dgot.at[h, s], send_d.at[h, s], recv_d.at[h, s], "dp", partner(bit)
        )

    for h in range(2):
        swap(h, 0).start()
    smine[...] = square
    sgot[me] = square
    for d in range(1, count):
        to_peer(d, smine, sgot, send_s, recv_s).start()
    for s in range(stages):
        for h in range(2):
            swap(h, s).wait_recv()
            pay[h, s + 1] = pay[h, s] + dgot[h, s]
            if s + 1 < stages:
                swap(h, s + 1).start()
    for h in range(2):
        fired_ref[h * half : (h + 1) * half, :] = pay[h, stages, :half, :]
    fired_heads_ref[...] = pay[0, stages, half:, :GROUP]
    for d in range(1, count):
        from_peer(d, smine, sgot, send_s, recv_s).wait_recv()
    total = sgot[0]
    for n in range(1, count):
        total = total + sgot[n]
    off = summed - last_heads_ref[...]
    line = total[0:1, :] + jnp.sum(off * off, axis=0, keepdims=True)
    line = jnp.broadcast_to(jnp.sum(line, axis=1, keepdims=True), square_ref.shape)
    square_ref[...] = jnp.sqrt(line + 1e-06)

    for s in range(stages):
        for h in range(2):
            swap(h, s).wait_send()
    for d in range(1, count):
        to_peer(d, hmine, hgot, send_h, recv_h).wait_send()
        to_peer(d, smine, sgot, send_s, recv_s).wait_send()

    def drain(j, unused):
        @pl.when(j >= (me + 1) * parts)
        def _():
            remote(block(j), got_r.at[j], send_r.at[j], recv_r.at[j], "seq", me + 1).wait_send()

        @pl.when(j < me * parts)
        def _():
            remote(block(j), got_l.at[j], send_l.at[j], recv_l.at[j], "seq", me - 1).wait_send()

        return unused

    lax.fori_loop(0, count * parts, drain, 0)


def local(
    count, replicas, tokens, values, out_grad, w_bc, w_dt, a_log, dt_bias, fire_flags,
    last_bc, last_heads, total_bc, total_heads,
):
    tok = tokens[0]
    x = values[0]
    g = out_grad[0]
    length, inner = x.shape
    heads = a_log.shape[0]
    width = inner // heads
    chunks = inner // LANES
    wide = w_bc.shape[1]
    half = wide // 2
    blocks = length // GROUP
    npairs = blocks * (blocks + 1) // 2
    sds = jax.ShapeDtypeStruct
    whole = lambda a: pl.BlockSpec(a.shape, lambda k: (0,) * len(a.shape))
    per = next(n for n in (4, 2, 1) if chunks % n == 0)
    chunk2 = pl.BlockSpec((length, per * LANES), lambda k: (0, k))
    chunk3 = pl.BlockSpec((per, half, LANES), lambda k: (k, 0, 0))
    small = sds((length, heads), F32)
    states = sds((chunks, half, LANES), F32)
    outs = [states, states, sds((chunks, 1, LANES), F32), sds((length, wide), F32)] + [small] * 4
    alog2 = a_log[None]
    bias2 = dt_bias[None]
    wdt = w_dt.T
    pair = pltpu.VMEM((2, length, 2 * heads), BF16)
    fresh, entry, decay, proj, cum, rate, sigcum, sig = pl.pallas_call(
        functools.partial(front_kernel, width),
        grid=(chunks // per,),
        in_specs=[whole(tok), whole(w_bc), whole(wdt), whole(alog2), whole(bias2), chunk2, chunk2],
        out_specs=[chunk3, chunk3, pl.BlockSpec((per, 1, LANES), lambda k: (k, 0, 0))]
        + [whole(o) for o in outs[3:]],
        out_shape=outs,
        scratch_shapes=[pair, pltpu.VMEM((2, wide, length), BF16)],
        name="front",
    )(tok, w_bc, wdt, alog2, bias2, x, g)
    vm = pl.BlockSpec(memory_space=pltpu.VMEM)
    buf = pltpu.VMEM((chunks, half, LANES), F32)
    sem = pltpu.SemaphoreType.DMA((chunks,))
    square_tiles = pltpu.VMEM((npairs, GROUP, GROUP), F32)
    head_rows = pltpu.VMEM((heads, GROUP), F32)
    d_projected, grad_heads = pl.pallas_call(
        functools.partial(chain_kernel, count, width),
        in_specs=[vm] * 10,
        out_specs=[vm, vm],
        out_shape=[sds((length, wide), BF16), sds((8, GROUP), F32)],
        scratch_shapes=[
            buf, buf, buf, buf, pair, pltpu.VMEM((2, length, wide), BF16),
            pltpu.VMEM((length, heads), F32),
            pltpu.VMEM((length, heads), F32),
            pltpu.VMEM((8, heads), F32),
            pltpu.VMEM((length, wide), F32),
            pltpu.VMEM((length, 3 * heads), BF16),
            pltpu.VMEM((length, 2 * heads), BF16),
            pltpu.VMEM((4, heads, length), F32),
            square_tiles, square_tiles, head_rows, head_rows,
            sem, sem, sem, sem,
        ],
        compiler_params=pltpu.CompilerParams(
            collective_id=0, has_side_effects=True, vmem_limit_bytes=56 * 1024 * 1024
        ),
        name="chain",
    )(decay, fresh, entry, x, g, proj, cum, rate, sigcum, sig)
    own_last = last_bc[0]
    rows = own_last.shape[0]
    stages = replicas.bit_length() - 1
    tile = lambda a: jnp.pad(a, ((0, 8 - a.shape[0]), (0, GROUP - a.shape[1])))
    weight = jnp.broadcast_to(fire_flags[0].astype(F32), (8, wide))
    dma = pltpu.SemaphoreType.DMA
    parts = 2 if rows % 16 == 0 else 1
    own_rows, fired_bc, summed, fired, square = pl.pallas_call(
        functools.partial(tail_kernel, count, replicas),
        in_specs=[vm] * 6,
        out_specs=[vm] * 5,
        out_shape=[sds((rows, wide), F32)] * 2 + [sds((8, GROUP), F32)] * 3,
        scratch_shapes=[
            pltpu.VMEM((rows * count, wide), F32),
            pltpu.VMEM((count * parts, rows // parts, wide), F32),
            pltpu.VMEM((count * parts, rows // parts, wide), F32),
            pltpu.VMEM((2, stages + 1, rows // 2 + 8, wide), F32),
            pltpu.VMEM((2, stages, rows // 2 + 8, wide), F32),
            pltpu.VMEM((count, 8, GROUP), F32),
            pltpu.VMEM((8, GROUP), F32),
            pltpu.VMEM((count, 8, GROUP), F32),
            pltpu.VMEM((8, GROUP), F32),
        ]
        + [dma((count * parts,))] * 4 + [dma((2, stages))] * 2 + [dma((count,))] * 4,
        compiler_params=pltpu.CompilerParams(
            collective_id=1, has_side_effects=True, vmem_limit_bytes=48 * 1024 * 1024
        ),
        name="tail",
    )(tok, d_projected, grad_heads, own_last, tile(last_heads[0]), weight)
    summed_heads = summed[:2, :heads]
    new_total_bc = total_bc + fired_bc
    new_total_heads = total_heads + fired[:2, :heads]
    new_last_bc = jnp.where(fire_flags[0] > 0, own_rows, own_last)[None]
    new_last_heads = jnp.where(fire_flags[0] > 0, summed_heads, last_heads[0])[None]
    return (new_total_bc, new_total_heads, new_last_bc, new_last_heads, square[0, :1])


def solution(mesh):
    in_specs = (
        P("dp", "seq", None), P("dp", "seq", None), P("dp", "seq", None), P(), P(), P(), P(),
        P("dp"), P("dp", "seq", None), P("dp", None, None), P("seq", None), P(),
    )
    out_specs = (P("seq", None), P(), P("dp", "seq", None), P("dp", None, None), P("dp"))
    return jax.shard_map(
        functools.partial(local, mesh.shape["seq"], mesh.shape["dp"]), mesh=mesh, in_specs=in_specs,
        out_specs=out_specs, check_vma=False,
    )
```
